32 devices in a mesh: grp: 2 (over core), kv: 2 (over x), srv: 8 (over z, y).
Axes of the slice: x: 2, y: 2, z: 4, core: 2. Of those that a mesh axis runs over, the one named last changes fastest.
Arguments:
- queries: bfloat16 [2048, 8, 1024], P('srv', 'kv', 'grp'), may hold values from -120 to 120
- keys: bfloat16 [2048, 8, 128], P('srv', 'kv'), may hold values from -5 to 5
- values: bfloat16 [2048, 8, 128], P('srv', 'kv'), may hold values from -6 to 6
- lengths: int32 [4], replicated, may hold values from 1 to 1024, 2048 in all
- output_projection_weight: bfloat16 [8, 1024, 8192], P('kv', 'grp', 'srv'), may hold values from -0.0625 to 0.0625
Outputs:
- projected: bfloat16 [2048, 8192], P('srv', ('grp', 'kv'))
The draws below stay inside these ranges and needn't reach their ends.
Inputs may be any that keep to these rules, and one draw needn't show every extreme that they name: The 4 lengths sum to 2048; the longest document has exactly 1024 tokens.
All inputs are finite; a program needn't handle non-finite values.
Results may differ from the reference program's by a relative error of at most 0.017.
Values may be sent and summed in bfloat16 or wider, within the bound.
A program may use at most 128 MiB of HBM per device.

```python
import math
import jax
import jax.numpy as jnp
import numpy as np
from jax import lax

MODEL_WIDTH = 8192
QUERY_HEADS = 64
KEY_VALUE_HEADS = 8
HEAD_WIDTH = 128
TOK_DEV = 256
QUERY_PER_KEY = 8
PACK_TOKENS = 2048
MOST = 1024
DOCS = 4
N_GRP = 2
N_KV = 2
N_SRV = 8


def shared_draw(key):
    base = jax.random.fold_in(key, 1234)
    key_random_seed, query_random_seed = jax.random.split(base, 2)
    key_tensor = jnp.clip(jax.random.normal(key_random_seed, (PACK_TOKENS, KEY_VALUE_HEADS, HEAD_WIDTH), jnp.float32), -5.0, 5.0)
    query_tensor = jnp.clip(jax.random.normal(query_random_seed, (PACK_TOKENS, KEY_VALUE_HEADS, QUERY_PER_KEY * HEAD_WIDTH), jnp.float32), -5.0, 5.0)
    return (query_tensor, key_tensor)


def draw_queries(key, part):
    return shared_draw(key)[0].astype(jnp.bfloat16)


def draw_keys(key, part):
    return shared_draw(key)[1].astype(jnp.bfloat16)


def levels(key, dims, shards, least, high):
    def one(dim, parts):
        heights = jax.random.uniform(jax.random.fold_in(jax.random.fold_in(key, 6), dim), (parts,), jnp.float32, least / len(shards), high / len(shards))
        return jnp.repeat(jnp.exp(heights), dims[dim] // parts).reshape((-1,) + (1,) * (len(dims) - dim - 1))

    factor_of = one(*shards[0])
    for cut in shards[1:]:
        factor_of = factor_of * one(*cut)
    return factor_of


def length_profile(count, total, reach, skew):
    portions = [(1 << 20) // math.isqrt(standing ** skew) + 1 for standing in range(2, count + 1)]
    surplus, given = total - reach - (count - 1), [1] * (count - 1)
    while surplus > 0:
        candidates = [i for i in range(count - 1) if given[i] < reach]
        whole, budget = sum([portions[i] for i in candidates]), surplus
        for i in candidates:
            more = min(reach - given[i], max(1, budget * portions[i] // whole), surplus)
            given[i] = given[i] + more
            surplus = surplus - more
    return np.array([reach] + given)


def uneven_parts(own_key, amount, total, most, slope):
    if amount == 2:
        one = jax.random.randint(own_key, (), max(1, total - most), min(most, total - 1) + 1)
        return jnp.stack([one, total - one])
    tallies = jnp.asarray(length_profile(amount, total, most, slope), jnp.int32)
    couples = (amount - 1) // 2
    giver, receiver = tallies[1:1 + 2 * couples:2], tallies[2:2 + 2 * couples:2]
    margin = jnp.minimum(giver - 1, most - receiver)
    shifted = jax.random.randint(jax.random.fold_in(own_key, 1), (couples,), 0, 1 << 20) % (margin + 1)
    tallies = tallies.at[1:1 + 2 * couples:2].set(giver - shifted).at[2:2 + 2 * couples:2].set(receiver + shifted)
    return tallies[jax.random.permutation(jax.random.fold_in(own_key, 2), amount)]


def normal_values(rng, shape, deviation, bound, cuts=(), held_as=jnp.bfloat16):
    result = deviation * jax.random.normal(rng, shape, jnp.float32)
    if cuts:
        result = result * levels(rng, shape, cuts, -0.22, 0.18)
    return jnp.clip(result, -bound, bound).astype(held_as)


def setup_inputs(seed: int = 0) -> dict:
    key_list = jax.random.split(jax.random.key(seed), 6)
    return {
        "queries": draw_queries(jax.random.fold_in(key_list[5], 71), 0),
        "keys": draw_keys(jax.random.fold_in(key_list[5], 71), 0),
        "values": normal_values(key_list[2], (PACK_TOKENS, KEY_VALUE_HEADS, HEAD_WIDTH), 1.0, 6.0, ((0, 8), (1, 2))),
        "lengths": uneven_parts(key_list[3], DOCS, PACK_TOKENS, MOST, 2).astype(jnp.int32),
        "output_projection_weight": normal_values(key_list[4], (KEY_VALUE_HEADS, QUERY_PER_KEY * HEAD_WIDTH, MODEL_WIDTH), (QUERY_HEADS * HEAD_WIDTH) ** -0.5, 0.0625, ((0, 2), (1, 2), (2, 8))),
    }


def doc_starts(lengths, position):
    starts = jnp.cumsum(lengths) - lengths
    chosen = jnp.where(starts[None, :] <= position[:, None], starts[None, :], 0)
    return lax.optimization_barrier(jnp.max(chosen, axis=1))

def attend_exact(query_block_rows, window_keys, window_values, query_pos, key_pos, lengths):
    token_count = query_block_rows.shape[0]
    split_output = query_block_rows.astype(jnp.float32).reshape(token_count, KEY_VALUE_HEADS, QUERY_PER_KEY, HEAD_WIDTH)
    scores = jnp.einsum('tjhd,wjd->jhtw', split_output, window_keys.astype(jnp.float32)) * (1.0 / math.sqrt(HEAD_WIDTH))
    first_key = doc_starts(lengths, query_pos)
    allowed = (key_pos[None, :] >= first_key[:, None]) & (key_pos[None, :] <= query_pos[:, None])
    scores = jnp.where(allowed[None, None], scores, -jnp.inf)
    peak = lax.optimization_barrier(jnp.max(scores, axis=3, keepdims=True))
    weights = jnp.exp(scores - peak)
    total = lax.optimization_barrier(jnp.sum(weights, axis=3))
    rounded = lax.optimization_barrier(weights.astype(jnp.bfloat16))
    numer = jnp.einsum('jhtw,wjd->tjhd', rounded.astype(jnp.float32), window_values.astype(jnp.float32))
    final_output = numer / jnp.transpose(total, (2, 0, 1))[..., None]
    return final_output.astype(jnp.bfloat16).reshape(token_count, KEY_VALUE_HEADS, QUERY_PER_KEY * HEAD_WIDTH)

def reference(queries, keys, values, lengths, output_projection_weight):
    window = MOST + TOK_DEV
    keys_padded = jnp.pad(keys, ((MOST, 0), (0, 0), (0, 0)))
    values_padded = jnp.pad(values, ((MOST, 0), (0, 0), (0, 0)))

    def one_block(index):
        start = index * TOK_DEV
        query_block_rows = lax.dynamic_slice_in_dim(queries, start, TOK_DEV, 0)
        window_keys = lax.dynamic_slice_in_dim(keys_padded, start, window, 0)
        window_values = lax.dynamic_slice_in_dim(values_padded, start, window, 0)
        query_pos = start + jnp.arange(TOK_DEV, dtype=jnp.int32)
        key_pos = start - MOST + jnp.arange(window, dtype=jnp.int32)
        return attend_exact(query_block_rows, window_keys, window_values, query_pos, key_pos, lengths)
    block_list = lax.map(one_block, jnp.arange(N_SRV, dtype=jnp.int32))
    attention_output = block_list.reshape(PACK_TOKENS, KEY_VALUE_HEADS, QUERY_PER_KEY * HEAD_WIDTH)
    heads_per_group = KEY_VALUE_HEADS // N_KV
    half_width = QUERY_PER_KEY * HEAD_WIDTH // N_GRP
    attended_split = attention_output.reshape(PACK_TOKENS, N_KV, heads_per_group, N_GRP, half_width)
    weight_split = output_projection_weight.reshape(N_KV, heads_per_group, N_GRP, half_width, MODEL_WIDTH)
    summed = jnp.zeros((PACK_TOKENS, MODEL_WIDTH), jnp.float32)
    for half_index in range(N_GRP):
        for group_index in range(N_KV):
            left = attended_split[:, group_index, :, half_index, :].reshape(PACK_TOKENS, heads_per_group * half_width)
            right = weight_split[group_index, :, half_index].reshape(heads_per_group * half_width, MODEL_WIDTH)
            partial_sum = jnp.dot(left, right, preferred_element_type=jnp.float32).astype(jnp.bfloat16)
            partial_sum = lax.optimization_barrier(partial_sum)
            summed = summed + partial_sum.astype(jnp.float32)
    return summed.astype(jnp.bfloat16)
```

```python
import functools
import math

import jax
import jax.numpy as jnp
from jax import lax
from jax.experimental import pallas as pl
from jax.experimental.pallas import tpu as pltpu
from jax.sharding import PartitionSpec as P

REACH = 4
EARLY = 2
FAR = -1e30
MESH = pl.DeviceIdType.MESH


def layer(plan, lengths, q_ref, kv_ref, w_ref, out_ref, kvw, qbuf, bias, abuf, wbuf, acc,
          send1, recv1, send2, recv2, send3, recv3, send4,
          ky_s, ky_r, kz_s, kz_r, sw_s, sw_r, q_s, q_r, own_w, w_s, w_r, a_s, a_r,
          s1, r1, s2, r2, s3, r3, s4, r4):
    head, heads, kvh, hp, hpp, halves, lanes, pairs, cw = plan
    tokens = q_ref.shape[0]
    inner = hp * head
    width = kvh * head
    split_kv = kv_ref.shape[2] > width
    own_chunks = w_ref.shape[1] // cw
    chunks = own_chunks * pairs
    items = lanes * pairs * chunks
    early = EARLY * pairs * own_chunks
    back = REACH // pairs
    half_pieces = hp // hpp
    pieces = half_pieces * pairs
    piece = hpp * head
    lag = min(4, pieces)
    per_kv = hp // kvh
    part = tokens // lanes
    a, g, s = lax.axis_index("grp"), lax.axis_index("kv"), lax.axis_index("srv")
    u, v = s // pairs, s % pairs
    q = a * halves + g
    ov = 1 - v

    core = (1 - a, g, s)
    beside = (a, g, u * pairs + ov)
    ahead = (a, g, s + pairs)
    behind = (a, g, s - pairs)
    right, left = u + 1 < lanes, u > 0
    at_home = q == u

    def other_half(k):
        return (a, (g + k) % halves, s)

    def owner(p):
        return (u // halves, u % halves, p * pairs + v)

    def giver(p):
        return (p // halves, p % halves, q * pairs + v)

    barrier = pltpu.get_barrier_semaphore()

    def greet(device):
        pl.semaphore_signal(barrier, inc=1, device_id=device, device_id_type=MESH)

    greet(core)
    greet(beside)
    for k in range(1, halves):
        greet(other_half(k))
    pl.when(right)(lambda: greet(ahead))
    pl.when(left)(lambda: greet(behind))
    for p in range(lanes):
        pl.when(jnp.logical_not(at_home & (q == p)))(lambda p=p: greet(giver(p)))
    peers = jnp.int32(1 + halves + lanes)
    peers = peers + jnp.where(right, 1, 0) + jnp.where(left, 1, 0) - jnp.where(at_home, 1, 0)

    def remote(src, dst, send, recv, device):
        return pltpu.make_async_remote_copy(
            src_ref=src, dst_ref=dst, send_sem=send, recv_sem=recv,
            device_id=device, device_id_type=MESH,
        )

    def lane_at(i, size):
        return pl.ds(pl.multiple_of(i, head), size)

    def kv_from(half, j):
        offset = half * width + j * head if split_kv else j * head
        return kv_ref.at[a, :, lane_at(offset, head)]

    def kv_at(m, back_by, w, j):
        return kvw.at[m, (back - back_by) * pairs + w, :, pl.ds(j * head, head)]

    def whose(w):
        return v if w == 0 else ov

    def kv_beside(j):
        return remote(kv_from(ov, j), kv_at(a, 0, v, j), ky_s.at[j], ky_r.at[j], beside)

    def kv_came(j):
        return remote(kv_from(ov, j), kv_at(a, 0, ov, j), ky_s.at[j], ky_r.at[j], beside)

    def kv_up(d, w, j):
        src = kv_from(v, j) if d == 1 and w == 0 else kv_at(a, d - 1, whose(w), j)
        return remote(src, kv_at(a, d, whose(w), j), kz_s.at[d - 1, w, j], kz_r.at[d - 1, w, j],
                      ahead)

    def swap(d, w, j, m):
        i = 0 if d == 0 else 2 * d - 1 + w
        ref = kv_at(m, d, whose(w), j)
        return remote(ref, ref, sw_s.at[i, j], sw_r.at[i, j], core)

    def query(j):
        size = per_kv * head
        return remote(q_ref.at[:, lane_at(ov * inner + j * size, size)],
                      qbuf.at[0, :, pl.ds(j * size, size)], q_s.at[j], q_r.at[j], beside)

    def weight(c):
        return remote(w_ref.at[pl.ds(ov * inner, inner), pl.ds(c * cw, cw)],
                      wbuf.at[own_chunks + c], w_s.at[c], w_r.at[c], beside)

    def own_weight(c):
        return pltpu.make_async_copy(
            w_ref.at[pl.ds(v * inner, inner), pl.ds(c * cw, cw)], wbuf.at[c], own_w.at[c])

    for c in range(own_chunks):
        own_weight(c).start()

    pl.semaphore_wait(barrier, peers)

    for j in range(kvh):
        kv_beside(j).start()
        pl.when(right)(lambda j=j: kv_up(1, 0, j).start())
        query(j).start()
    for c in range(own_chunks):
        weight(c).start()

    for m in range(2):
        offset = v * width if split_kv else 0
        kvw[m, back * pairs + v] = kv_ref[m, :, lane_at(offset, width)]
    qbuf[1] = q_ref[:, lane_at(v * inner, inner)]
    for d in range(1, back + 1):
        @pl.when(u < d)
        def _():
            for m in range(2):
                for w in range(pairs):
                    kvw[m, (back - d) * pairs + w] = jnp.zeros((tokens, width), kvw.dtype)

    row = lax.broadcasted_iota(jnp.int32, (tokens, 1), 0)
    lane = lax.broadcasted_iota(jnp.int32, (tokens, tokens), 1)
    for h in range(pairs):
        shard = u * pairs + (ov if h == 0 else v)
        query_pos = shard * tokens + row
        first = jnp.zeros((tokens, 1), jnp.int32)
        start = jnp.int32(0)
        for i in range(lengths.shape[0]):
            first = jnp.where(query_pos >= start, start, first)
            start = start + lengths[i]
        for d in range(REACH + 1):
            key_pos = (shard - REACH + d) * tokens + lane
            allowed = (key_pos >= first) & (key_pos <= query_pos)
            bias[h, :, d * tokens:(d + 1) * tokens] = jnp.where(allowed, 0.0, FAR)

    def kv_phase(j):
        kv_came(j).wait_recv()
        pl.when(right)(lambda: kv_up(1, 1, j).start())
        swap(0, 1, j, a).start()
        for d in range(1, back + 1):
            @pl.when(u >= d)
            def _():
                for w in range(pairs):
                    kv_up(d, w, j).wait_recv()
                    if d < back:
                        pl.when(right)(lambda w=w: kv_up(d + 1, w, j).start())
                    swap(d, w, j, a).start()

    def kv_ready(j):
        swap(0, 1, j, 1 - a).wait_recv()
        for d in range(1, back + 1):
            @pl.when(u >= d)
            def _():
                for w in range(pairs):
                    swap(d, w, j, 1 - a).wait_recv()

    def bit(p, i):
        h, r = i // half_pieces, i % half_pieces
        return abuf.at[p, jnp.where(h == 0, ov, v), :, lane_at(r * piece, piece)]

    def relay(way, d, i):
        p = u - (d - 1) if way == 0 else u + (d - 1)
        return remote(bit(p, i), bit(p, i), a_s.at[way, d - 1, i], a_r.at[way, d - 1, i],
                      ahead if way == 0 else behind)

    def relayed(way, d, i):
        p = u - d if way == 0 else u + d
        return remote(bit(p, i), bit(p, i), a_s.at[way, d - 1, i], a_r.at[way, d - 1, i],
                      behind if way == 0 else ahead)

    def holds(way, d):
        return u >= d if way == 0 else u + d < lanes

    def may_send(way):
        return right if way == 0 else left

    def forward(d, i):
        for way in range(2):
            @pl.when(holds(way, d - 1) & may_send(way))
            def _():
                relayed(way, d - 1, i).wait_recv()
                relay(way, d, i).start()

    factor = math.log2(math.e) / math.sqrt(head)
    kv_phase(0)
    kv_ready(0)

    def per_unit(i, carry):
        h, hh = i // hp, i % hp
        vv = jnp.where(h == 0, ov, v)
        for j in range(kvh):
            if j > 0:
                pl.when(i == (j - 1) * per_kv + min(2, per_kv - 1))(lambda: kv_phase(j))
                pl.when(i == j * per_kv)(lambda: kv_ready(j))
            pl.when(i == j * per_kv)(lambda: query(j).wait_recv())
        mine = lane_at(hh * head, head)
        at = lane_at((hh // heads) * head, head)
        window = kvw[0, pl.ds(vv, REACH + 1), :, at].reshape((REACH + 1) * tokens, head)
        scores = lax.dot_general(
            qbuf[h, :, mine], window, (((1,), (1,)), ((), ())),
            preferred_element_type=jnp.float32,
        ) + bias[h]
        peak = jnp.max(scores, axis=1, keepdims=True)
        weights = jnp.exp2((scores - peak) * factor)
        total = jnp.sum(weights, axis=1, keepdims=True)
        numer = jnp.dot(
            weights.astype(jnp.bfloat16),
            kvw[1, pl.ds(vv, REACH + 1), :, at].reshape((REACH + 1) * tokens, head),
            preferred_element_type=jnp.float32,
        )
        abuf[u, vv, :, mine] = (numer / total).astype(abuf.dtype)

        @pl.when(i % hpp == hpp - 1)
        def _():
            n = i // hpp
            for way in range(2):
                pl.when(may_send(way))(lambda: relay(way, 1, n).start())
            pl.when(n >= lag)(lambda: forward(2, n - lag))

        return carry

    lax.fori_loop(0, hp * pairs, per_unit, 0)

    def plane(k):
        low = jnp.minimum(u, lanes - 1 - u)
        zigzag = jnp.where(k % 2 == 1, u - (k + 1) // 2, u + k // 2)
        line = jnp.where(u < lanes - 1 - u, k, lanes - 1 - k)
        return jnp.where(k <= 2 * low, zigzag, line)

    def decode(n):
        m = n - early
        r = n - EARLY * pairs * chunks
        late = n >= EARLY * pairs * chunks
        first = n < early
        k = jnp.where(first, n // (pairs * own_chunks),
                      jnp.where(late, EARLY + r // (pairs * chunks), m % (pairs * EARLY) // pairs))
        h = jnp.where(first, n // own_chunks % pairs,
                      jnp.where(late, r // chunks % pairs, m % pairs))
        c = jnp.where(first, n % own_chunks,
                      jnp.where(late, r % chunks, own_chunks + m // (pairs * EARLY)))
        return k, h, c

    def column(c):
        return jnp.where(c < own_chunks, v * own_chunks + c, ov * own_chunks + c - own_chunks)

    def to_core(n):
        return remote(send1.at[n], recv1.at[n], s1.at[n], r1.at[n], core)

    def to_half(n, k):
        rows = pl.ds((g + k) % halves * part, part)
        return remote(send2.at[n, rows], recv2.at[n, k - 1], s2.at[n], r2.at[n], other_half(k))

    def all_halves(n):
        return remote(recv2.at[n], recv2.at[n], s2.at[n], r2.at[n], other_half(1))

    def to_beside(k, c):
        return remote(send3.at[k, c], recv3.at[k, c], s3.at[k, c], r3.at[k, c], beside)

    def result(giver_index, c):
        return out_ref.at[pl.ds(giver_index * part, part), lane_at(c * cw, cw)]

    def to_owner(k, c):
        return remote(send4.at[k, c], result(q, c), s4.at[k, c], r4.at[q, c], owner(plane(k)))

    def to_self(c):
        return pltpu.make_async_copy(send4.at[0, c], result(q, c), r4.at[q, c])

    def given(p, c):
        return remote(send4.at[0, c], result(p, c), s4.at[0, c], r4.at[p, c], giver(p))

    def stage1(n):
        k, h, c = decode(n)
        product = jnp.dot(abuf[plane(k), jnp.where(h == 0, ov, v)], wbuf[c],
                          preferred_element_type=jnp.float32)
        low, high = product[:tokens // 2], product[tokens // 2:]
        acc[n] = jnp.where(a == 0, low, high)
        send1[n] = jnp.where(a == 0, high, low).astype(send1.dtype)
        to_core(n).start()

    def stage2(n):
        to_core(n).wait_recv()
        total = acc[n] + recv1[n].astype(jnp.float32)
        acc[n] = total
        send2[n] = total.astype(send2.dtype)
        for k in range(1, halves):
            to_half(n, k).start()

    kept = pl.ds(g * part, part)

    def stage3(n):
        k, h, c = decode(n)
        if halves > 1:
            all_halves(n).wait_recv()
        total = acc[n, kept]
        for i in range(halves - 1):
            total = total + recv2[n, i].astype(jnp.float32)

        @pl.when(h == 0)
        def _():
            send3[k, column(c)] = total.astype(send3.dtype)
            to_beside(k, column(c)).start()

        @pl.when(h != 0)
        def _():
            acc[n, kept] = total

    def stage4(n, k, c):
        col = column(c)
        to_beside(k, col).wait_recv()
        total = acc[n, kept] + recv3[k, col].astype(jnp.float32)
        send4[k, col] = total.astype(send4.dtype)
        pl.when(at_home & (k == 0))(lambda: to_self(col).start())
        pl.when(jnp.logical_not(at_home & (k == 0)))(lambda: to_owner(k, col).start())

    def arrived(k, h):
        p = plane(k)
        up = p < u
        d = jnp.where(up, u - p, p - u)
        way = jnp.where(up, 0, 1)

        @pl.when(jnp.logical_not(jnp.where(up, right, left)))
        def _():
            def one(r, carry):
                i = h * half_pieces + r
                remote(bit(p, i), bit(p, i), a_s.at[way, d - 1, i], a_r.at[way, d - 1, i],
                       core).wait_recv()
                return carry

            lax.fori_loop(0, half_pieces, one, 0)

    first_end = EARLY * chunks

    def per_item(n, carry):
        k, h, c = decode(n)
        pl.when(n < lag)(lambda: forward(2, pieces - lag + n))
        if lanes > 3:
            pl.when((n >= lag) & (n < lag + pieces))(lambda: forward(3, n - lag))
        if lanes > 4:
            @pl.when(n == lag + pieces)
            def _():
                for d in range(4, lanes):
                    def one(i, carry):
                        forward(d, i)
                        return carry

                    lax.fori_loop(0, pieces, one, 0)

        for i in range(own_chunks):
            pl.when(n == i)(lambda i=i: own_weight(i).wait())
            pl.when(n == early + i * pairs * EARLY)(lambda i=i: weight(i).wait_recv())
        fresh = (n < items) & (c == 0) & (k > 0) & (h < pairs)

        @pl.when(fresh)
        def _():
            stage2(n - 1)
            arrived(k, h)

        pl.when(n < items)(lambda: stage1(n))
        pl.when(jnp.logical_not(fresh) & (n >= 1) & (n <= items))(lambda: stage2(n - 1))
        pl.when((n >= 3) & (n < items + 3))(lambda: stage3(n - 3))
        m = n - (first_end + EARLY * own_chunks + 2)

        @pl.when((m >= 0) & (m < first_end))
        def _():
            mk, mc = m // chunks, m % chunks
            index = jnp.where(mc < own_chunks, mk * pairs * own_chunks + own_chunks + mc,
                              early + (mc - own_chunks) * pairs * EARLY + mk * pairs + 1)
            stage4(index, mk, mc)

        lk, lh, lc = decode(n - 4)
        pl.when((n - 4 >= EARLY * pairs * chunks) & (lh == 1))(lambda: stage4(n - 4, lk, lc))
        return carry

    lax.fori_loop(0, items + 4, per_item, 0)

    for j in range(kvh):
        kv_beside(j).wait_send()
        query(j).wait_send()
        swap(0, 1, j, a).wait_send()
        for d in range(1, back + 1):
            for w in range(pairs):
                pl.when((u >= d - 1) & right)(lambda d=d, w=w, j=j: kv_up(d, w, j).wait_send())
                pl.when(u >= d)(lambda d=d, w=w, j=j: swap(d, w, j, a).wait_send())
    for c in range(own_chunks):
        weight(c).wait_send()
    for d in range(1, lanes):
        for way in range(2):
            @pl.when(holds(way, d - 1) & may_send(way))
            def _():
                def one(i, carry):
                    relay(way, d, i).wait_send()
                    return carry

                lax.fori_loop(0, pieces, one, 0)

    def sent(n, carry):
        to_core(n).wait_send()
        if halves > 1:
            all_halves(n).wait_send()
        return carry

    lax.fori_loop(0, items, sent, 0)

    def finish(i, carry):
        k, c = i // chunks, i % chunks
        to_beside(k, c).wait_send()
        pl.when(jnp.logical_not(at_home & (k == 0)))(lambda: to_owner(k, c).wait_send())
        pl.when(at_home & (k == q))(lambda: to_self(c).wait())
        pl.when(jnp.logical_not(at_home & (k == q)))(lambda: given(k, c).wait_recv())
        return carry

    lax.fori_loop(0, lanes * chunks, finish, 0)


def on_device(queries, keys, values, lengths, output_projection_weight):
    tokens = queries.shape[0]
    cores, halves = lax.axis_size("grp"), lax.axis_size("kv")
    lanes = cores * halves
    pairs = lax.axis_size("srv") // lanes
    assert cores == 2 and pairs == 2 and lanes > 2
    q = queries.reshape(tokens, -1)
    kv = jnp.stack([keys.reshape(tokens, -1), values.reshape(tokens, -1)])
    groups, head = keys.shape[1], keys.shape[2]
    inner = q.shape[1]
    weight = output_projection_weight.reshape(inner, -1)
    columns = weight.shape[1]
    heads = inner // (groups * head)
    kvh = max(1, groups // pairs)
    hp = inner // head // pairs
    hpp = 2
    cw = max(256, columns // 2)
    own_chunks = columns // cw
    chunks = own_chunks * pairs
    items = lanes * pairs * chunks
    pieces = hp // hpp * pairs
    part = tokens // lanes
    back = REACH // pairs
    width = kvh * head
    dma = pltpu.SemaphoreType.DMA
    bf16, f32 = jnp.bfloat16, jnp.float32
    vmem = pl.BlockSpec(memory_space=pltpu.VMEM)
    return pl.pallas_call(
        functools.partial(layer, (head, heads, kvh, hp, hpp, halves, lanes, pairs, cw)),
        out_shape=jax.ShapeDtypeStruct((tokens, pairs * columns), bf16),
        in_specs=[
            pl.BlockSpec(memory_space=pltpu.SMEM), vmem, vmem,
            pl.BlockSpec(memory_space=pl.ANY),
        ],
        out_specs=pl.BlockSpec(memory_space=pl.ANY),
        scratch_shapes=[
            pltpu.VMEM((2, (back + 1) * pairs, tokens, width), bf16),
            pltpu.VMEM((pairs, tokens, hp * head), bf16),
            pltpu.VMEM((pairs, tokens, (REACH + 1) * tokens), f32),
            pltpu.VMEM((lanes, pairs, tokens, hp * head), bf16),
            pltpu.VMEM((chunks, hp * head, cw), bf16),
            pltpu.VMEM((items, tokens // cores, cw), f32),
            pltpu.VMEM((items, tokens // cores, cw), bf16),
            pltpu.VMEM((items, tokens // cores, cw), bf16),
            pltpu.VMEM((items, tokens // cores, cw), bf16),
            pltpu.VMEM((items, halves - 1, part, cw), bf16),
            pltpu.VMEM((lanes, chunks, part, cw), bf16),
            pltpu.VMEM((lanes, chunks, part, cw), bf16),
            pltpu.VMEM((lanes, chunks, part, cw), bf16),
            dma((kvh,)), dma((kvh,)), dma((back, pairs, kvh)), dma((back, pairs, kvh)),
            dma((2 * back + 1, kvh)), dma((2 * back + 1, kvh)), dma((kvh,)), dma((kvh,)),
            dma((own_chunks,)), dma((own_chunks,)), dma((own_chunks,)),
            dma((2, lanes - 1, pieces)), dma((2, lanes - 1, pieces)),
            dma((items,)), dma((items,)), dma((items,)), dma((items,)),
            dma((lanes, chunks)), dma((lanes, chunks)), dma((lanes, chunks)), dma((lanes, chunks)),
        ],
        compiler_params=pltpu.CompilerParams(
            collective_id=0, has_side_effects=True, vmem_limit_bytes=60 * 1024 * 1024
        ),
    )(lengths, q, kv, weight)


def solution(mesh):
    placed = (
        P("srv", "kv", "grp"),
        P("srv", "kv", None),
        P("srv", "kv", None),
        P(),
        P("kv", "grp", "srv"),
    )
    return jax.shard_map(
        on_device, mesh=mesh, in_specs=placed, out_specs=P("srv", ("grp", "kv")), check_vma=False
    )
```

```python
import functools
import math

import jax
import jax.numpy as jnp
from jax import lax
from jax.experimental import pallas as pl
from jax.experimental.pallas import tpu as pltpu
from jax.sharding import PartitionSpec as P

REACH = 4
EARLY = 3
FAR = -1e30
LAG = 5
MESH = pl.DeviceIdType.MESH


def layer(plan, lengths, q_ref, kv_ref, w_ref, out_ref, kvw, qbuf, bias, abuf, wbuf, acc,
          send1, recv1, send2, recv2, send3, recv3, far3, send4,
          ky_s, ky_r, kz_s, kz_r, sw_s, sw_r, q_s, q_r, own_w, w_s, w_r, a_s, a_r,
          s1, r1, s2, r2, s3, r3, s4, r4):
    head, heads, kvh, hp, hpp, halves, lanes, pairs, cw = plan
    tokens = q_ref.shape[0]
    inner = hp * head
    width = kvh * head
    split_kv = kv_ref.shape[2] > width
    own_chunks = w_ref.shape[1] // cw
    chunks = own_chunks * pairs
    items = lanes * pairs * chunks
    soon = own_chunks // 2
    segments = [(0, 2, 0, own_chunks), (0, 2, own_chunks, soon), (2, 1, 0, own_chunks + soon),
                (0, EARLY, own_chunks + soon, own_chunks - soon),
                (EARLY, lanes - EARLY, 0, chunks)]
    starts = [0]
    for _, planes, _, some in segments:
        starts.append(starts[-1] + planes * pairs * some)
    places = {}
    for (k0, planes, c0, some), n0 in zip(segments[:-1], starts):
        for r in range(planes * pairs * some):
            places[k0 + r // (pairs * some), r // some % pairs, c0 + r % some] = n0 + r
    swapped = (lanes - EARLY) * pairs * chunks
    ordered = [c for c in range(chunks) if c % own_chunks >= soon]
    ordered = ordered + [c for c in range(chunks) if c not in ordered]
    partner = [(c + own_chunks) % chunks for c in ordered]
    last = [[(k, c) for k in range(EARLY) for c in range(chunks) if (c % own_chunks < soon) == kind]
            for kind in (True, False)]
    settle = [
        max([max(places[k, 1, c], places[k, 0, (c + own_chunks) % chunks]) + LAG + 1 - m
             for m, (k, c) in enumerate(some)] + [starts[3] + 2])
        for some in last
    ]
    settle.append(settle[1] + swapped)
    settle[1] = max(settle[1], settle[0] + len(last[0]))
    settle[2] = max(settle[2], settle[0] + len(last[0]))
    back = REACH // pairs
    pieces = hp // hpp * pairs
    piece = hpp * head
    per_kv = hp // kvh
    per_run = per_kv // hpp
    each = -(-pieces // 3)
    wait_for = own_chunks * pairs - 1 if own_chunks > 1 else 0
    part = tokens // lanes
    a, g, s = lax.axis_index("grp"), lax.axis_index("kv"), lax.axis_index("srv")
    u, v = s // pairs, s % pairs
    q = a * halves + g
    ov = 1 - v

    core = (1 - a, g, s)
    beside = (a, g, u * pairs + ov)
    ahead = (a, g, s + pairs)
    behind = (a, g, s - pairs)
    right, left = u + 1 < lanes, u > 0
    at_home = q == u

    def other_half(k):
        return (a, (g + k) % halves, s)

    def owner(p):
        return (u // halves, u % halves, p * pairs + v)

    def giver(p):
        return (p // halves, p % halves, q * pairs + v)

    barrier = pltpu.get_barrier_semaphore()

    def greet(device):
        pl.semaphore_signal(barrier, inc=1, device_id=device, device_id_type=MESH)

    greet(core)
    greet(beside)
    for k in range(1, halves):
        greet(other_half(k))
    pl.when(right)(lambda: greet(ahead))
    pl.when(left)(lambda: greet(behind))
    for p in range(lanes):
        pl.when(jnp.logical_not(at_home & (q == p)))(lambda p=p: greet(giver(p)))
    peers = jnp.int32(1 + halves + lanes)
    peers = peers + jnp.where(right, 1, 0) + jnp.where(left, 1, 0) - jnp.where(at_home, 1, 0)

    def remote(src, dst, send, recv, device):
        return pltpu.make_async_remote_copy(
            src_ref=src, dst_ref=dst, send_sem=send, recv_sem=recv,
            device_id=device, device_id_type=MESH,
        )

    def lane_at(i, size):
        return pl.ds(pl.multiple_of(i, head), size)

    def kv_from(half, j):
        offset = half * width + j * head if split_kv else j * head
        return kv_ref.at[a, :, lane_at(offset, head)]

    def kv_at(m, back_by, w, j):
        return kvw.at[m, (back - back_by) * pairs + w, :, pl.ds(j * head, head)]

    def whose(w):
        return v if w == 0 else ov

    def kv_beside(j):
        return remote(kv_from(ov, j), kv_at(a, 0, v, j), ky_s.at[j], ky_r.at[j], beside)

    def kv_came(j):
        return remote(kv_from(ov, j), kv_at(a, 0, ov, j), ky_s.at[j], ky_r.at[j], beside)

    def kv_up(d, w, j):
        src = kv_from(v, j) if d == 1 and w == 0 else kv_at(a, d - 1, whose(w), j)
        return remote(src, kv_at(a, d, whose(w), j), kz_s.at[d - 1, w, j], kz_r.at[d - 1, w, j],
                      ahead)

    def swap(d, w, j, m):
        i = 0 if d == 0 else 2 * d - 1 + w
        ref = kv_at(m, d, whose(w), j)
        return remote(ref, ref, sw_s.at[i, j], sw_r.at[i, j], core)

    def query(j):
        size = per_kv * head
        return remote(q_ref.at[:, lane_at(ov * inner + j * size, size)],
                      qbuf.at[0, :, pl.ds(j * size, size)], q_s.at[j], q_r.at[j], beside)

    def weight(c):
        return remote(w_ref.at[pl.ds(ov * inner, inner), pl.ds(c * cw, cw)],
                      wbuf.at[own_chunks + c], w_s.at[c], w_r.at[c], beside)

    def own_weight(c):
        return pltpu.make_async_copy(
            w_ref.at[pl.ds(v * inner, inner), pl.ds(c * cw, cw)], wbuf.at[c], own_w.at[c])

    for c in range(own_chunks):
        own_weight(c).start()

    pl.semaphore_wait(barrier, peers)

    for j in range(kvh):
        kv_beside(j).start()
        pl.when(right)(lambda j=j: kv_up(1, 0, j).start())
    for j in range(kvh):
        query(j).start()
    for c in range(own_chunks):
        weight(c).start()

    for m in range(2):
        offset = v * width if split_kv else 0
        kvw[m, back * pairs + v] = kv_ref[m, :, lane_at(offset, width)]
    qbuf[1] = q_ref[:, lane_at(v * inner, inner)]
    for d in range(1, back + 1):
        @pl.when(u < d)
        def _():
            for m in range(2):
                for w in range(pairs):
                    kvw[m, (back - d) * pairs + w] = jnp.zeros((tokens, width), kvw.dtype)

    row = lax.broadcasted_iota(jnp.int32, (tokens, 1), 0)
    lane = lax.broadcasted_iota(jnp.int32, (tokens, tokens), 1)
    for h in range(pairs):
        shard = u * pairs + (ov if h == 0 else v)
        query_pos = shard * tokens + row
        first = jnp.zeros((tokens, 1), jnp.int32)
        start = jnp.int32(0)
        for i in range(lengths.shape[0]):
            first = jnp.where(query_pos >= start, start, first)
            start = start + lengths[i]
        for d in range(REACH + 1):
            key_pos = (shard - REACH + d) * tokens + lane
            allowed = (key_pos >= first) & (key_pos <= query_pos)
            bias[h, :, d * tokens:(d + 1) * tokens] = jnp.where(allowed, 0.0, FAR)

    def kv_hop(d, j):
        @pl.when(u >= d)
        def _():
            for w in range(pairs):
                kv_up(d, w, j).wait_recv()
                if d < back:
                    pl.when(right)(lambda w=w: kv_up(d + 1, w, j).start())
                swap(d, w, j, a).start()

    def kv_phase(j):
        kv_came(j).wait_recv()
        pl.when(right)(lambda: kv_up(1, 1, j).start())
        swap(0, 1, j, a).start()
        for d in range(1, back):
            kv_hop(d, j)

    def kv_ready(j):
        swap(0, 1, j, 1 - a).wait_recv()
        for d in range(1, back + 1):
            @pl.when(u >= d)
            def _():
                for w in range(pairs):
                    swap(d, w, j, 1 - a).wait_recv()

    def run(b):
        other = (b >= 1) & (b <= kvh)
        h = jnp.where(other, 0, 1)
        j = jnp.where(b <= 1, 0, jnp.where(other, b - 1, b - kvh))
        return h, j

    def bit(p, i):
        h, j = run(i // per_run)
        r = j * per_run + i % per_run
        return abuf.at[p, jnp.where(h == 0, ov, v), :, lane_at(r * piece, piece)]

    def relay(way, d, i):
        p = u - (d - 1) if way == 0 else u + (d - 1)
        return remote(bit(p, i), bit(p, i), a_s.at[way, d - 1, i], a_r.at[way, d - 1, i],
                      ahead if way == 0 else behind)

    def relayed(way, d, i):
        p = u - d if way == 0 else u + d
        return remote(bit(p, i), bit(p, i), a_s.at[way, d - 1, i], a_r.at[way, d - 1, i],
                      behind if way == 0 else ahead)

    def holds(way, d):
        return u >= d if way == 0 else u + d < lanes

    def may_send(way):
        return right if way == 0 else left

    def forward(d, i):
        for way in range(2):
            @pl.when(holds(way, d - 1) & may_send(way))
            def _():
                relayed(way, d - 1, i).wait_recv()
                relay(way, d, i).start()

    factor = math.log2(math.e) / math.sqrt(head)
    for j in range(min(2, kvh)):
        kv_phase(j)
    kv_hop(back, 0)
    kv_ready(0)

    def per_unit(i):
        h, kj = run(i // per_kv)
        hh = kj * per_kv + i % per_kv
        vv = jnp.where(h == 0, ov, v)
        for j in range(kvh):
            if j > 0:
                if j > 1:
                    pl.when(i == (j - 1) * per_kv)(lambda: kv_phase(j))
                pl.when(i == (j + 1) * per_kv - 1)(lambda: kv_hop(back, j))
                pl.when(i == (j + 1) * per_kv)(lambda: kv_ready(j))
            pl.when(i == (j + 1) * per_kv)(lambda: query(j).wait_recv())
        mine = lane_at(hh * head, head)
        at = lane_at(kj * head, head)
        window = kvw[0, pl.ds(vv, REACH + 1), :, at].reshape((REACH + 1) * tokens, head)
        scores = lax.dot_general(
            qbuf[h, :, mine], window, (((1,), (1,)), ((), ())),
            preferred_element_type=jnp.float32,
        ) + bias[h]
        peak = jnp.max(scores, axis=1, keepdims=True)
        weights = jnp.exp2((scores - peak) * factor)
        total = jnp.sum(weights, axis=1, keepdims=True)
        numer = jnp.dot(
            weights.astype(jnp.bfloat16),
            kvw[1, pl.ds(vv, REACH + 1), :, at].reshape((REACH + 1) * tokens, head),
            preferred_element_type=jnp.float32,
        )
        abuf[u, vv, :, mine] = (numer / total).astype(abuf.dtype)

        @pl.when(i % hpp == hpp - 1)
        def _():
            n = i // hpp
            for way in range(2):
                pl.when(may_send(way))(lambda: relay(way, 1, n).start())

    units = hp * pairs
    ahead_by = units - own_chunks - 1

    def plane(k):
        low = jnp.minimum(u, lanes - 1 - u)
        zigzag = jnp.where(k % 2 == 1, u - (k + 1) // 2, u + k // 2)
        line = jnp.where(u < lanes - 1 - u, k, lanes - 1 - k)
        return jnp.where(k <= 2 * low, zigzag, line)

    inside = left & right

    def pick(i, values):
        found = jnp.int32(values[0])
        for at, value in enumerate(values[1:], 1):
            found = jnp.where(i == at, value, found)
        return found

    def decode(n):
        k, h, c = jnp.int32(0), jnp.int32(0), jnp.int32(0)
        fresh = jnp.bool_(False)
        kept_in = n < items
        m = jnp.where(n < starts[3] + swapped, n + starts[4] - starts[3], n - swapped)
        n = jnp.where(inside & (n >= starts[3]) & (n < items), m, n)
        for (k0, planes, c0, some), n0 in zip(segments, starts):
            if planes * some == 0:
                continue
            r = n - n0
            here = r >= 0
            half, order = r // some % pairs, c0 + r % some
            if k0 == EARLY:
                order = jnp.where(half == 0, pick(r % some, ordered), pick(r % some, partner))
            k = jnp.where(here, k0 + r // (pairs * some), k)
            h = jnp.where(here, half, h)
            c = jnp.where(here, order, c)
            fresh = jnp.where(here, (r % some == 0) & (c0 == 0), fresh)
        return k, h, c, fresh & (k > 0) & kept_in

    def column(c):
        return jnp.where(c < own_chunks, v * own_chunks + c, ov * own_chunks + c - own_chunks)

    def to_core(n):
        return remote(send1.at[n], recv1.at[n], s1.at[n], r1.at[n], core)

    def to_half(n, k):
        rows = pl.ds((g + k) % halves * part, part)
        return remote(send2.at[n, rows], recv2.at[n, k - 1], s2.at[n], r2.at[n], other_half(k))

    def all_halves(n):
        return remote(recv2.at[n], recv2.at[n], s2.at[n], r2.at[n], other_half(1))

    def to_beside(k, c):
        return remote(send3.at[k, c], recv3.at[k, c], s3.at[k, c], r3.at[k, c], beside)

    def result(giver_index, c):
        return out_ref.at[pl.ds(giver_index * part, part), lane_at(c * cw, cw)]

    def to_owner(k, c):
        return remote(send4.at[k, c], result(q, c), s4.at[k, c], r4.at[q, c], owner(plane(k)))

    def to_self(c):
        return pltpu.make_async_copy(send4.at[0, c], result(q, c), r4.at[q, c])

    def given(p, c):
        return remote(send4.at[0, c], result(p, c), s4.at[0, c], r4.at[p, c], giver(p))

    def stage1(n):
        k, h, c, _ = decode(n)
        product = jnp.dot(abuf[plane(k), jnp.where(h == 0, ov, v)], wbuf[c],
                          preferred_element_type=jnp.float32)
        low, high = product[:tokens // 2], product[tokens // 2:]
        acc[n] = jnp.where(a == 0, low, high)
        send1[n] = jnp.where(a == 0, high, low).astype(send1.dtype)
        to_core(n).start()

    def far_beside(k, c, n):
        return remote(send2.at[n], far3.at[k - EARLY, c], s3.at[k, c], r3.at[k, c], beside)

    def to_halves(n, total):
        acc[n] = total
        send2[n] = total.astype(send2.dtype)
        for k in range(1, halves):
            to_half(n, k).start()

    def direct(k, c):
        return (k >= EARLY) & (c % own_chunks >= soon)

    def stage2(n):
        k, h, c, _ = decode(n)
        col = column(c)
        to_core(n).wait_recv()
        total = acc[n] + recv1[n].astype(jnp.float32)
        y_first = direct(k, c)
        pl.when(jnp.logical_not(y_first))(lambda: to_halves(n, total))

        @pl.when(y_first & (h == 0))
        def _():
            send2[n] = total.astype(send2.dtype)
            far_beside(k, col, n).start()

        @pl.when(y_first & (h != 0))
        def _():
            far_beside(k, col, n).wait_recv()
            to_halves(n, total + far3[k - EARLY, col].astype(jnp.float32))

    kept = pl.ds(g * part, part)

    def deliver(k, col, total):
        send4[k, col] = total.astype(send4.dtype)
        pl.when(at_home & (k == 0))(lambda: to_self(col).start())
        pl.when(jnp.logical_not(at_home & (k == 0)))(lambda: to_owner(k, col).start())

    def stage3(n):
        k, h, c, _ = decode(n)
        col = column(c)

        y_first = direct(k, c)

        @pl.when(jnp.logical_not(y_first) | (h != 0))
        def _():
            all_halves(n).wait_recv()
            total = acc[n, kept]
            for i in range(halves - 1):
                total = total + recv2[n, i].astype(jnp.float32)

            @pl.when(h == 0)
            def _():
                send3[k, col] = total.astype(send3.dtype)
                to_beside(k, col).start()

            @pl.when((h != 0) & (k < EARLY))
            def _():
                acc[n, kept] = total

            pl.when((h != 0) & y_first)(lambda: deliver(k, col, total))

            @pl.when((h != 0) & (k >= EARLY) & jnp.logical_not(y_first))
            def _():
                to_beside(k, col).wait_recv()
                deliver(k, col, total + recv3[k, col].astype(jnp.float32))

    def stage4(n, k, c):
        col = column(c)
        to_beside(k, col).wait_recv()
        deliver(k, col, acc[n, kept] + recv3[k, col].astype(jnp.float32))

    def arrived(k, h):
        p = plane(k)
        up = p < u
        d = jnp.where(up, u - p, p - u)
        way = jnp.where(up, 0, 1)

        @pl.when(jnp.logical_not(jnp.where(up, right, left)))
        def _():
            def one(r, carry):
                i = jnp.where(h == 0, per_run + r,
                              jnp.where(r < per_run, r, r + kvh * per_run))
                remote(bit(p, i), bit(p, i), a_s.at[way, d - 1, i], a_r.at[way, d - 1, i],
                       core).wait_recv()
                return carry

            lax.fori_loop(0, kvh * per_run, one, 0)

    def per_item(n):
        k, h, c, fresh = decode(n)

        f = (n - wait_for) * each

        @pl.when((f >= 0) & (f < pieces))
        def _():
            for i in range(each):
                pl.when(f + i < pieces)(lambda i=i: forward(2, f + i))

        if lanes > 3:
            for i in range(pieces):
                at = starts[1] + (starts[3] - starts[1] + 1) * i // pieces
                pl.when(n == at)(lambda i=i: forward(3, i))
        if lanes > 4:
            @pl.when(n == starts[3])
            def _():
                for d in range(4, lanes):
                    def one(i, carry):
                        forward(d, i)
                        return carry

                    lax.fori_loop(0, pieces, one, 0)

        for i in range(own_chunks):
            used = starts[1] + i if i < soon else starts[3]
            pl.when(n == i)(lambda i=i: own_weight(i).wait())
            pl.when(n == used)(lambda i=i: weight(i).wait_recv())
        done = decode(n - 1)[3]
        pl.when(fresh & jnp.logical_not(done) & (n >= 2))(lambda: stage2(n - 2))

        @pl.when(fresh)
        def _():
            stage2(n - 1)
            arrived(k, h)

        pl.when(n < items)(lambda: stage1(n))
        pending = jnp.logical_not(fresh | done) & (n >= 2) & (n < items + 2)
        pl.when(pending)(lambda: stage2(n - 2))
        pl.when((n >= LAG) & (n < items + LAG))(lambda: stage3(n - LAG))
        later = jnp.where(inside, swapped, 0)
        index, mk, mc = jnp.int32(-1), jnp.int32(0), jnp.int32(0)
        begins = settle[0], jnp.where(inside, settle[2], settle[1])
        for some, first, shift in zip(last, begins, (0, later)):
            for m, (k1, c1) in enumerate(some):
                here = n == first + m
                held = places[k1, 1, c1]
                index = jnp.where(here, held + (shift if held >= starts[3] else 0), index)
                mk, mc = jnp.where(here, k1, mk), jnp.where(here, c1, mc)
        pl.when(index >= 0)(lambda: stage4(index, mk, mc))

    def step(i, carry):
        pl.when(i < units)(lambda: per_unit(i))
        pl.when(i >= ahead_by)(lambda: per_item(i - ahead_by))
        return carry

    lax.fori_loop(0, ahead_by + max(items + LAG, settle[2] + len(last[1])), step, 0)

    for j in range(kvh):
        kv_beside(j).wait_send()
        query(j).wait_send()
        swap(0, 1, j, a).wait_send()
        for d in range(1, back + 1):
            for w in range(pairs):
                pl.when((u >= d - 1) & right)(lambda d=d, w=w, j=j: kv_up(d, w, j).wait_send())
                pl.when(u >= d)(lambda d=d, w=w, j=j: swap(d, w, j, a).wait_send())
    for c in range(own_chunks):
        weight(c).wait_send()
    for d in range(1, lanes):
        for way in range(2):
            @pl.when(holds(way, d - 1) & may_send(way))
            def _():
                def one(i, carry):
                    relay(way, d, i).wait_send()
                    return carry

                lax.fori_loop(0, pieces, one, 0)

    def sent(n, carry):
        k, h, c, _ = decode(n)
        to_core(n).wait_send()
        near = jnp.logical_not(direct(k, c)) | (h != 0)
        pl.when(near)(lambda: all_halves(n).wait_send())
        pl.when(jnp.logical_not(near))(lambda: far_beside(k, column(c), n).wait_send())
        return carry

    lax.fori_loop(0, items, sent, 0)

    def finish(i, carry):
        k, c = i // chunks, i % chunks
        y_first = (k >= EARLY) & (c % own_chunks >= soon)
        pl.when(jnp.logical_not(y_first))(lambda: to_beside(k, c).wait_send())
        pl.when(jnp.logical_not(at_home & (k == 0)))(lambda: to_owner(k, c).wait_send())
        pl.when(at_home & (k == q))(lambda: to_self(c).wait())
        pl.when(jnp.logical_not(at_home & (k == q)))(lambda: given(k, c).wait_recv())
        return carry

    lax.fori_loop(0, lanes * chunks, finish, 0)


def on_device(queries, keys, values, lengths, output_projection_weight):
    tokens = queries.shape[0]
    cores, halves = lax.axis_size("grp"), lax.axis_size("kv")
    lanes = cores * halves
    pairs = lax.axis_size("srv") // lanes
    assert cores == 2 and pairs == 2 and halves > 1 and lanes > EARLY
    q = queries.reshape(tokens, -1)
    kv = jnp.stack([keys.reshape(tokens, -1), values.reshape(tokens, -1)])
    groups, head = keys.shape[1], keys.shape[2]
    inner = q.shape[1]
    weight = output_projection_weight.reshape(inner, -1)
    columns = weight.shape[1]
    heads = inner // (groups * head)
    kvh = max(1, groups // pairs)
    hp = inner // head // pairs
    hpp = 2
    cw = max(256, columns // 2)
    own_chunks = columns // cw
    chunks = own_chunks * pairs
    items = lanes * pairs * chunks
    pieces = hp // hpp * pairs
    part = tokens // lanes
    back = REACH // pairs
    width = kvh * head
    dma = pltpu.SemaphoreType.DMA
    bf16, f32 = jnp.bfloat16, jnp.float32
    vmem = pl.BlockSpec(memory_space=pltpu.VMEM)
    return pl.pallas_call(
        functools.partial(layer, (head, heads, kvh, hp, hpp, halves, lanes, pairs, cw)),
        out_shape=jax.ShapeDtypeStruct((tokens, pairs * columns), bf16),
        in_specs=[
            pl.BlockSpec(memory_space=pltpu.SMEM), vmem, vmem,
            pl.BlockSpec(memory_space=pl.ANY),
        ],
        out_specs=pl.BlockSpec(memory_space=pl.ANY),
        scratch_shapes=[
            pltpu.VMEM((2, (back + 1) * pairs, tokens, width), bf16),
            pltpu.VMEM((pairs, tokens, hp * head), bf16),
            pltpu.VMEM((pairs, tokens, (REACH + 1) * tokens), f32),
            pltpu.VMEM((lanes, pairs, tokens, hp * head), bf16),
            pltpu.VMEM((chunks, hp * head, cw), bf16),
            pltpu.VMEM((items, tokens // cores, cw), f32),
            pltpu.VMEM((items, tokens // cores, cw), bf16),
            pltpu.VMEM((items, tokens // cores, cw), bf16),
            pltpu.VMEM((items, tokens // cores, cw), bf16),
            pltpu.VMEM((items, halves - 1, part, cw), bf16),
            pltpu.VMEM((lanes, chunks, part, cw), bf16),
            pltpu.VMEM((lanes, chunks, part, cw), bf16),
            pltpu.VMEM((lanes - EARLY, chunks, tokens // cores, cw), bf16),
            pltpu.VMEM((lanes, chunks, part, cw), bf16),
            dma((kvh,)), dma((kvh,)), dma((back, pairs, kvh)), dma((back, pairs, kvh)),
            dma((2 * back + 1, kvh)), dma((2 * back + 1, kvh)), dma((kvh,)), dma((kvh,)),
            dma((own_chunks,)), dma((own_chunks,)), dma((own_chunks,)),
            dma((2, lanes - 1, pieces)), dma((2, lanes - 1, pieces)),
            dma((items,)), dma((items,)), dma((items,)), dma((items,)),
            dma((lanes, chunks)), dma((lanes, chunks)), dma((lanes, chunks)), dma((lanes, chunks)),
        ],
        compiler_params=pltpu.CompilerParams(
            collective_id=0, has_side_effects=True, vmem_limit_bytes=60 * 1024 * 1024
        ),
    )(lengths, q, kv, weight)


def solution(mesh):
    placed = (
        P("srv", "kv", "grp"),
        P("srv", "kv", None),
        P("srv", "kv", None),
        P(),
        P("kv", "grp", "srv"),
    )
    return jax.shard_map(
        on_device, mesh=mesh, in_specs=placed, out_specs=P("srv", ("grp", "kv")), check_vma=False
    )
```

```python
import functools
import math

import jax
import jax.numpy as jnp
from jax import lax
from jax.experimental import pallas as pl
from jax.experimental.pallas import tpu as pltpu
from jax.sharding import PartitionSpec as P

REACH = 4
EARLY = 3
FAR = -1e30
LAG = 5
MESH = pl.DeviceIdType.MESH


def layer(plan, lengths_in, q_hbm, k_hbm, v_hbm, w_ref, out_ref,
          lengths, q_in, k_in, v_in, q_ref, kv_ref, kvw, qbuf, bias, abuf, wbuf, acc,
          send1, recv1, send2, recv2, send3, recv3, far3, send4,
          ky_s, ky_r, kz_s, kz_r, sw_s, sw_r, q_s, q_r, own_w, w_s, w_r, a_s, a_r,
          s1, r1, s2, r2, s3, r3, s4, r4, in_s):
    head, heads, kvh, hp, hpp, halves, lanes, pairs, cw = plan
    tokens = q_ref.shape[0]
    inner = hp * head
    width = kvh * head
    split_kv = kv_ref.shape[2] > width
    own_chunks = w_ref.shape[1] // cw
    chunks = own_chunks * pairs
    items = lanes * pairs * chunks
    soon = own_chunks // 2
    segments = [(0, 2, 0, own_chunks), (0, 2, own_chunks, soon), (2, 1, 0, own_chunks + soon),
                (0, EARLY, own_chunks + soon, own_chunks - soon),
                (EARLY, lanes - EARLY, 0, chunks)]
    starts = [0]
    for _, planes, _, some in segments:
        starts.append(starts[-1] + planes * pairs * some)
    places = {}
    for (k0, planes, c0, some), n0 in zip(segments[:-1], starts):
        for r in range(planes * pairs * some):
            places[k0 + r // (pairs * some), r // some % pairs, c0 + r % some] = n0 + r
    swapped = (lanes - EARLY) * pairs * chunks
    ordered = [c for c in range(chunks) if c % own_chunks >= soon]
    ordered = ordered + [c for c in range(chunks) if c not in ordered]
    partner = [(c + own_chunks) % chunks for c in ordered]
    last = [[(k, c) for k in range(EARLY) for c in range(chunks) if (c % own_chunks < soon) == kind]
            for kind in (True, False)]
    settle = [
        max([max(places[k, 1, c], places[k, 0, (c + own_chunks) % chunks]) + LAG + 1 - m
             for m, (k, c) in enumerate(some)] + [starts[3] + 2])
        for some in last
    ]
    settle.append(settle[1] + swapped)
    settle[1] = max(settle[1], settle[0] + len(last[0]))
    settle[2] = max(settle[2], settle[0] + len(last[0]))
    back = REACH // pairs
    pieces = hp // hpp * pairs
    piece = hpp * head
    per_kv = hp // kvh
    per_run = per_kv // hpp
    each = -(-pieces // 3)
    wait_for = own_chunks * pairs - 1 if own_chunks > 1 else 0
    part = tokens // lanes
    a, g, s = lax.axis_index("grp"), lax.axis_index("kv"), lax.axis_index("srv")
    u, v = s // pairs, s % pairs
    q = a * halves + g
    ov = 1 - v

    core = (1 - a, g, s)
    beside = (a, g, u * pairs + ov)
    ahead = (a, g, s + pairs)
    behind = (a, g, s - pairs)
    right, left = u + 1 < lanes, u > 0
    at_home = q == u

    def other_half(k):
        return (a, (g + k) % halves, s)

    def owner(p):
        return (u // halves, u % halves, p * pairs + v)

    def giver(p):
        return (p // halves, p % halves, q * pairs + v)

    arriving = [
        pltpu.make_async_copy(src, dst, in_s.at[i])
        for i, (src, dst) in enumerate(
            ((k_hbm, k_in), (v_hbm, v_in), (q_hbm, q_in), (lengths_in, lengths)))
    ]
    for copy in arriving:
        copy.start()

    barrier = pltpu.get_barrier_semaphore()

    def greet(device):
        pl.semaphore_signal(barrier, inc=1, device_id=device, device_id_type=MESH)

    greet(core)
    greet(beside)
    for k in range(1, halves):
        greet(other_half(k))
    pl.when(right)(lambda: greet(ahead))
    pl.when(left)(lambda: greet(behind))
    for p in range(lanes):
        pl.when(jnp.logical_not(at_home & (q == p)))(lambda p=p: greet(giver(p)))
    peers = jnp.int32(1 + halves + lanes)
    peers = peers + jnp.where(right, 1, 0) + jnp.where(left, 1, 0) - jnp.where(at_home, 1, 0)

    def remote(src, dst, send, recv, device):
        return pltpu.make_async_remote_copy(
            src_ref=src, dst_ref=dst, send_sem=send, recv_sem=recv,
            device_id=device, device_id_type=MESH,
        )

    def lane_at(i, size):
        return pl.ds(pl.multiple_of(i, head), size)

    def kv_from(half, j):
        offset = half * width + j * head if split_kv else j * head
        return kv_ref.at[a, :, lane_at(offset, head)]

    def kv_at(m, back_by, w, j):
        return kvw.at[m, (back - back_by) * pairs + w, :, pl.ds(j * head, head)]

    def whose(w):
        return v if w == 0 else ov

    def kv_beside(j):
        return remote(kv_from(ov, j), kv_at(a, 0, v, j), ky_s.at[j], ky_r.at[j], beside)

    def kv_came(j):
        return remote(kv_from(ov, j), kv_at(a, 0, ov, j), ky_s.at[j], ky_r.at[j], beside)

    def kv_up(d, w, j):
        src = kv_from(v, j) if d == 1 and w == 0 else kv_at(a, d - 1, whose(w), j)
        return remote(src, kv_at(a, d, whose(w), j), kz_s.at[d - 1, w, j], kz_r.at[d - 1, w, j],
                      ahead)

    def swap(d, w, j, m):
        i = 0 if d == 0 else 2 * d - 1 + w
        ref = kv_at(m, d, whose(w), j)
        return remote(ref, ref, sw_s.at[i, j], sw_r.at[i, j], core)

    def query(j):
        size = per_kv * head
        return remote(q_ref.at[:, lane_at(ov * inner + j * size, size)],
                      qbuf.at[0, :, pl.ds(j * size, size)], q_s.at[j], q_r.at[j], beside)

    def weight(c):
        return remote(w_ref.at[pl.ds(ov * inner, inner), pl.ds(c * cw, cw)],
                      wbuf.at[own_chunks + c], w_s.at[c], w_r.at[c], beside)

    def own_weight(c):
        return pltpu.make_async_copy(
            w_ref.at[pl.ds(v * inner, inner), pl.ds(c * cw, cw)], wbuf.at[c], own_w.at[c])

    for c in range(own_chunks):
        own_weight(c).start()

    arriving[0].wait()
    arriving[1].wait()
    for j in range(k_in.shape[1]):
        kv_ref[0, :, j * head:(j + 1) * head] = k_in[:, j]
        kv_ref[1, :, j * head:(j + 1) * head] = v_in[:, j]

    pl.semaphore_wait(barrier, peers)

    for j in range(kvh):
        kv_beside(j).start()
        pl.when(right)(lambda j=j: kv_up(1, 0, j).start())
    span = q_in.shape[2]
    arriving[2].wait()
    for j in range(q_in.shape[1]):
        q_ref[:, j * span:(j + 1) * span] = q_in[:, j]
    for j in range(kvh):
        query(j).start()
    for c in range(own_chunks):
        weight(c).start()

    for m in range(2):
        offset = v * width if split_kv else 0
        kvw[m, back * pairs + v] = kv_ref[m, :, lane_at(offset, width)]
    qbuf[1] = q_ref[:, lane_at(v * inner, inner)]
    for d in range(1, back + 1):
        @pl.when(u < d)
        def _():
            for m in range(2):
                for w in range(pairs):
                    kvw[m, (back - d) * pairs + w] = jnp.zeros((tokens, width), kvw.dtype)

    arriving[3].wait()
    row = lax.broadcasted_iota(jnp.int32, (tokens, 1), 0)
    lane = lax.broadcasted_iota(jnp.int32, (tokens, tokens), 1)
    for h in range(pairs):
        shard = u * pairs + (ov if h == 0 else v)
        query_pos = shard * tokens + row
        first = jnp.zeros((tokens, 1), jnp.int32)
        start = jnp.int32(0)
        for i in range(lengths.shape[0]):
            first = jnp.where(query_pos >= start, start, first)
            start = start + lengths[i]
        for d in range(REACH + 1):
            key_pos = (shard - REACH + d) * tokens + lane
            allowed = (key_pos >= first) & (key_pos <= query_pos)
            bias[h, :, d * tokens:(d + 1) * tokens] = jnp.where(allowed, 0.0, FAR)

    def kv_hop(d, j):
        @pl.when(u >= d)
        def _():
            for w in range(pairs):
                kv_up(d, w, j).wait_recv()
                if d < back:
                    pl.when(right)(lambda w=w: kv_up(d + 1, w, j).start())
                swap(d, w, j, a).start()

    def kv_phase(j):
        kv_came(j).wait_recv()
        pl.when(right)(lambda: kv_up(1, 1, j).start())
        swap(0, 1, j, a).start()
        for d in range(1, back):
            kv_hop(d, j)

    def kv_ready(j):
        swap(0, 1, j, 1 - a).wait_recv()
        for d in range(1, back + 1):
            @pl.when(u >= d)
            def _():
                for w in range(pairs):
                    swap(d, w, j, 1 - a).wait_recv()

    def run(b):
        other = (b >= 1) & (b <= kvh)
        h = jnp.where(other, 0, 1)
        j = jnp.where(b <= 1, 0, jnp.where(other, b - 1, b - kvh))
        return h, j

    def bit(p, i):
        h, j = run(i // per_run)
        r = j * per_run + i % per_run
        return abuf.at[p, jnp.where(h == 0, ov, v), :, lane_at(r * piece, piece)]

    def relay(way, d, i):
        p = u - (d - 1) if way == 0 else u + (d - 1)
        return remote(bit(p, i), bit(p, i), a_s.at[way, d - 1, i], a_r.at[way, d - 1, i],
                      ahead if way == 0 else behind)

    def relayed(way, d, i):
        p = u - d if way == 0 else u + d
        return remote(bit(p, i), bit(p, i), a_s.at[way, d - 1, i], a_r.at[way, d - 1, i],
                      behind if way == 0 else ahead)

    def holds(way, d):
        return u >= d if way == 0 else u + d < lanes

    def may_send(way):
        return right if way == 0 else left

    def forward(d, i):
        for way in range(2):
            @pl.when(holds(way, d - 1) & may_send(way))
            def _():
                relayed(way, d - 1, i).wait_recv()
                relay(way, d, i).start()

    factor = math.log2(math.e) / math.sqrt(head)
    for j in range(min(2, kvh)):
        kv_phase(j)
    kv_hop(back, 0)
    kv_ready(0)

    def per_unit(i):
        h, kj = run(i // per_kv)
        hh = kj * per_kv + i % per_kv
        vv = jnp.where(h == 0, ov, v)
        for j in range(kvh):
            if j > 0:
                if j > 1:
                    pl.when(i == (j - 1) * per_kv)(lambda: kv_phase(j))
                pl.when(i == (j + 1) * per_kv - 1)(lambda: kv_hop(back, j))
                pl.when(i == (j + 1) * per_kv)(lambda: kv_ready(j))
            pl.when(i == (j + 1) * per_kv)(lambda: query(j).wait_recv())
        mine = lane_at(hh * head, head)
        at = lane_at(kj * head, head)
        window = kvw[0, pl.ds(vv, REACH + 1), :, at].reshape((REACH + 1) * tokens, head)
        scores = lax.dot_general(
            qbuf[h, :, mine], window, (((1,), (1,)), ((), ())),
            preferred_element_type=jnp.float32,
        ) + bias[h]
        peak = jnp.max(scores, axis=1, keepdims=True)
        weights = jnp.exp2((scores - peak) * factor)
        total = jnp.sum(weights, axis=1, keepdims=True)
        numer = jnp.dot(
            weights.astype(jnp.bfloat16),
            kvw[1, pl.ds(vv, REACH + 1), :, at].reshape((REACH + 1) * tokens, head),
            preferred_element_type=jnp.float32,
        )
        abuf[u, vv, :, mine] = (numer / total).astype(abuf.dtype)

        @pl.when(i % hpp == hpp - 1)
        def _():
            n = i // hpp
            for way in range(2):
                pl.when(may_send(way))(lambda: relay(way, 1, n).start())

    units = hp * pairs
    ahead_by = units - own_chunks - 1

    def plane(k):
        low = jnp.minimum(u, lanes - 1 - u)
        zigzag = jnp.where(k % 2 == 1, u - (k + 1) // 2, u + k // 2)
        line = jnp.where(u < lanes - 1 - u, k, lanes - 1 - k)
        return jnp.where(k <= 2 * low, zigzag, line)

    inside = left & right

    def pick(i, values):
        found = jnp.int32(values[0])
        for at, value in enumerate(values[1:], 1):
            found = jnp.where(i == at, value, found)
        return found

    def decode(n):
        k, h, c = jnp.int32(0), jnp.int32(0), jnp.int32(0)
        fresh = jnp.bool_(False)
        kept_in = n < items
        m = jnp.where(n < starts[3] + swapped, n + starts[4] - starts[3], n - swapped)
        n = jnp.where(inside & (n >= starts[3]) & (n < items), m, n)
        for (k0, planes, c0, some), n0 in zip(segments, starts):
            if planes * some == 0:
                continue
            r = n - n0
            here = r >= 0
            half, order = r // some % pairs, c0 + r % some
            if k0 == EARLY:
                order = jnp.where(half == 0, pick(r % some, ordered), pick(r % some, partner))
            k = jnp.where(here, k0 + r // (pairs * some), k)
            h = jnp.where(here, half, h)
            c = jnp.where(here, order, c)
            fresh = jnp.where(here, (r % some == 0) & (c0 == 0), fresh)
        return k, h, c, fresh & (k > 0) & kept_in

    def column(c):
        return jnp.where(c < own_chunks, v * own_chunks + c, ov * own_chunks + c - own_chunks)

    def to_core(n):
        return remote(send1.at[n], recv1.at[n], s1.at[n], r1.at[n], core)

    def to_half(n, k):
        rows = pl.ds((g + k) % halves * part, part)
        return remote(send2.at[n, rows], recv2.at[n, k - 1], s2.at[n], r2.at[n], other_half(k))

    def all_halves(n):
        return remote(recv2.at[n], recv2.at[n], s2.at[n], r2.at[n], other_half(1))

    def to_beside(k, c):
        return remote(send3.at[k, c], recv3.at[k, c], s3.at[k, c], r3.at[k, c], beside)

    def result(giver_index, c):
        return out_ref.at[pl.ds(giver_index * part, part), lane_at(c * cw, cw)]

    def to_owner(k, c):
        return remote(send4.at[k, c], result(q, c), s4.at[k, c], r4.at[q, c], owner(plane(k)))

    def to_self(c):
        return pltpu.make_async_copy(send4.at[0, c], result(q, c), r4.at[q, c])

    def given(p, c):
        return remote(send4.at[0, c], result(p, c), s4.at[0, c], r4.at[p, c], giver(p))

    def stage1(n):
        k, h, c, _ = decode(n)
        product = jnp.dot(abuf[plane(k), jnp.where(h == 0, ov, v)], wbuf[c],
                          preferred_element_type=jnp.float32)
        low, high = product[:tokens // 2], product[tokens // 2:]
        acc[n] = jnp.where(a == 0, low, high)
        send1[n] = jnp.where(a == 0, high, low).astype(send1.dtype)
        to_core(n).start()

    def far_beside(k, c, n):
        return remote(send2.at[n], far3.at[k - EARLY, c], s3.at[k, c], r3.at[k, c], beside)

    def to_halves(n, total):
        acc[n] = total
        send2[n] = total.astype(send2.dtype)
        for k in range(1, halves):
            to_half(n, k).start()

    def direct(k, c):
        return (k >= EARLY) & (c % own_chunks >= soon)

    def stage2(n):
        k, h, c, _ = decode(n)
        col = column(c)
        to_core(n).wait_recv()
        total = acc[n] + recv1[n].astype(jnp.float32)
        y_first = direct(k, c)
        pl.when(jnp.logical_not(y_first))(lambda: to_halves(n, total))

        @pl.when(y_first & (h == 0))
        def _():
            send2[n] = total.astype(send2.dtype)
            far_beside(k, col, n).start()

        @pl.when(y_first & (h != 0))
        def _():
            far_beside(k, col, n).wait_recv()
            to_halves(n, total + far3[k - EARLY, col].astype(jnp.float32))

    kept = pl.ds(g * part, part)

    def deliver(k, col, total):
        send4[k, col] = total.astype(send4.dtype)
        pl.when(at_home & (k == 0))(lambda: to_self(col).start())
        pl.when(jnp.logical_not(at_home & (k == 0)))(lambda: to_owner(k, col).start())

    def stage3(n):
        k, h, c, _ = decode(n)
        col = column(c)

        y_first = direct(k, c)

        @pl.when(jnp.logical_not(y_first) | (h != 0))
        def _():
            all_halves(n).wait_recv()
            total = acc[n, kept]
            for i in range(halves - 1):
                total = total + recv2[n, i].astype(jnp.float32)

            @pl.when(h == 0)
            def _():
                send3[k, col] = total.astype(send3.dtype)
                to_beside(k, col).start()

            @pl.when((h != 0) & (k < EARLY))
            def _():
                acc[n, kept] = total

            pl.when((h != 0) & y_first)(lambda: deliver(k, col, total))

            @pl.when((h != 0) & (k >= EARLY) & jnp.logical_not(y_first))
            def _():
                to_beside(k, col).wait_recv()
                deliver(k, col, total + recv3[k, col].astype(jnp.float32))

    def stage4(n, k, c):
        col = column(c)
        to_beside(k, col).wait_recv()
        deliver(k, col, acc[n, kept] + recv3[k, col].astype(jnp.float32))

    def arrived(k, h):
        p = plane(k)
        up = p < u
        d = jnp.where(up, u - p, p - u)
        way = jnp.where(up, 0, 1)

        @pl.when(jnp.logical_not(jnp.where(up, right, left)))
        def _():
            def one(r, carry):
                i = jnp.where(h == 0, per_run + r,
                              jnp.where(r < per_run, r, r + kvh * per_run))
                remote(bit(p, i), bit(p, i), a_s.at[way, d - 1, i], a_r.at[way, d - 1, i],
                       core).wait_recv()
                return carry

            lax.fori_loop(0, kvh * per_run, one, 0)

    def per_item(n):
        k, h, c, fresh = decode(n)

        f = (n - wait_for) * each

        @pl.when((f >= 0) & (f < pieces))
        def _():
            for i in range(each):
                pl.when(f + i < pieces)(lambda i=i: forward(2, f + i))

        if lanes > 3:
            for i in range(pieces):
                at = starts[1] + (starts[3] - starts[1] + 1) * i // pieces
                pl.when(n == at)(lambda i=i: forward(3, i))
        if lanes > 4:
            @pl.when(n == starts[3])
            def _():
                for d in range(4, lanes):
                    def one(i, carry):
                        forward(d, i)
                        return carry

                    lax.fori_loop(0, pieces, one, 0)

        for i in range(own_chunks):
            used = starts[1] + i if i < soon else starts[3]
            pl.when(n == i)(lambda i=i: own_weight(i).wait())
            pl.when(n == used)(lambda i=i: weight(i).wait_recv())
        done = decode(n - 1)[3]
        pl.when(fresh & jnp.logical_not(done) & (n >= 2))(lambda: stage2(n - 2))

        @pl.when(fresh)
        def _():
            stage2(n - 1)
            arrived(k, h)

        pl.when(n < items)(lambda: stage1(n))
        pending = jnp.logical_not(fresh | done) & (n >= 2) & (n < items + 2)
        pl.when(pending)(lambda: stage2(n - 2))
        pl.when((n >= LAG) & (n < items + LAG))(lambda: stage3(n - LAG))
        later = jnp.where(inside, swapped, 0)
        index, mk, mc = jnp.int32(-1), jnp.int32(0), jnp.int32(0)
        begins = settle[0], jnp.where(inside, settle[2], settle[1])
        for some, first, shift in zip(last, begins, (0, later)):
            for m, (k1, c1) in enumerate(some):
                here = n == first + m
                held = places[k1, 1, c1]
                index = jnp.where(here, held + (shift if held >= starts[3] else 0), index)
                mk, mc = jnp.where(here, k1, mk), jnp.where(here, c1, mc)
        pl.when(index >= 0)(lambda: stage4(index, mk, mc))

    def step(i, carry):
        pl.when(i < units)(lambda: per_unit(i))
        pl.when(i >= ahead_by)(lambda: per_item(i - ahead_by))
        return carry

    lax.fori_loop(0, ahead_by + max(items + LAG, settle[2] + len(last[1])), step, 0)

    for j in range(kvh):
        kv_beside(j).wait_send()
        query(j).wait_send()
        swap(0, 1, j, a).wait_send()
        for d in range(1, back + 1):
            for w in range(pairs):
                pl.when((u >= d - 1) & right)(lambda d=d, w=w, j=j: kv_up(d, w, j).wait_send())
                pl.when(u >= d)(lambda d=d, w=w, j=j: swap(d, w, j, a).wait_send())
    for c in range(own_chunks):
        weight(c).wait_send()
    for d in range(1, lanes):
        for way in range(2):
            @pl.when(holds(way, d - 1) & may_send(way))
            def _():
                def one(i, carry):
                    relay(way, d, i).wait_send()
                    return carry

                lax.fori_loop(0, pieces, one, 0)

    def sent(n, carry):
        k, h, c, _ = decode(n)
        to_core(n).wait_send()
        near = jnp.logical_not(direct(k, c)) | (h != 0)
        pl.when(near)(lambda: all_halves(n).wait_send())
        pl.when(jnp.logical_not(near))(lambda: far_beside(k, column(c), n).wait_send())
        return carry

    lax.fori_loop(0, items, sent, 0)

    def finish(i, carry):
        k, c = i // chunks, i % chunks
        y_first = (k >= EARLY) & (c % own_chunks >= soon)
        pl.when(jnp.logical_not(y_first))(lambda: to_beside(k, c).wait_send())
        pl.when(jnp.logical_not(at_home & (k == 0)))(lambda: to_owner(k, c).wait_send())
        pl.when(at_home & (k == q))(lambda: to_self(c).wait())
        pl.when(jnp.logical_not(at_home & (k == q)))(lambda: given(k, c).wait_recv())
        return carry

    lax.fori_loop(0, lanes * chunks, finish, 0)


def on_device(queries, keys, values, lengths, output_projection_weight):
    tokens = queries.shape[0]
    cores, halves = lax.axis_size("grp"), lax.axis_size("kv")
    lanes = cores * halves
    pairs = lax.axis_size("srv") // lanes
    assert cores == 2 and pairs == 2 and halves > 1 and lanes > EARLY
    groups, head = keys.shape[1], keys.shape[2]
    inner = groups * queries.shape[2]
    weight = output_projection_weight.reshape(inner, -1)
    columns = weight.shape[1]
    heads = inner // (groups * head)
    kvh = max(1, groups // pairs)
    hp = inner // head // pairs
    hpp = 2
    cw = max(256, columns // 2)
    own_chunks = columns // cw
    chunks = own_chunks * pairs
    items = lanes * pairs * chunks
    pieces = hp // hpp * pairs
    part = tokens // lanes
    back = REACH // pairs
    width = kvh * head
    dma = pltpu.SemaphoreType.DMA
    bf16, f32 = jnp.bfloat16, jnp.float32
    hbm = pl.BlockSpec(memory_space=pltpu.HBM)
    return pl.pallas_call(
        functools.partial(layer, (head, heads, kvh, hp, hpp, halves, lanes, pairs, cw)),
        out_shape=jax.ShapeDtypeStruct((tokens, pairs * columns), bf16),
        in_specs=[hbm] * 5,
        out_specs=pl.BlockSpec(memory_space=pl.ANY),
        scratch_shapes=[
            pltpu.SMEM(lengths.shape, lengths.dtype),
            pltpu.VMEM(queries.shape, bf16),
            pltpu.VMEM(keys.shape, bf16),
            pltpu.VMEM(values.shape, bf16),
            pltpu.VMEM((tokens, inner), bf16),
            pltpu.VMEM((2, tokens, groups * head), bf16),
            pltpu.VMEM((2, (back + 1) * pairs, tokens, width), bf16),
            pltpu.VMEM((pairs, tokens, hp * head), bf16),
            pltpu.VMEM((pairs, tokens, (REACH + 1) * tokens), f32),
            pltpu.VMEM((lanes, pairs, tokens, hp * head), bf16),
            pltpu.VMEM((chunks, hp * head, cw), bf16),
            pltpu.VMEM((items, tokens // cores, cw), f32),
            pltpu.VMEM((items, tokens // cores, cw), bf16),
            pltpu.VMEM((items, tokens // cores, cw), bf16),
            pltpu.VMEM((items, tokens // cores, cw), bf16),
            pltpu.VMEM((items, halves - 1, part, cw), bf16),
            pltpu.VMEM((lanes, chunks, part, cw), bf16),
            pltpu.VMEM((lanes, chunks, part, cw), bf16),
            pltpu.VMEM((lanes - EARLY, chunks, tokens // cores, cw), bf16),
            pltpu.VMEM((lanes, chunks, part, cw), bf16),
            dma((kvh,)), dma((kvh,)), dma((back, pairs, kvh)), dma((back, pairs, kvh)),
            dma((2 * back + 1, kvh)), dma((2 * back + 1, kvh)), dma((kvh,)), dma((kvh,)),
            dma((own_chunks,)), dma((own_chunks,)), dma((own_chunks,)),
            dma((2, lanes - 1, pieces)), dma((2, lanes - 1, pieces)),
            dma((items,)), dma((items,)), dma((items,)), dma((items,)),
            dma((lanes, chunks)), dma((lanes, chunks)), dma((lanes, chunks)), dma((lanes, chunks)),
            dma((4,)),
        ],
        compiler_params=pltpu.CompilerParams(
            collective_id=0, has_side_effects=True, vmem_limit_bytes=52 * 1024 * 1024
        ),
    )(*[pltpu.with_memory_space_constraint(x, pltpu.HBM) for x in (lengths, queries, keys, values, weight)])


def solution(mesh):
    placed = (
        P("srv", "kv", "grp"),
        P("srv", "kv", None),
        P("srv", "kv", None),
        P(),
        P("kv", "grp", "srv"),
    )
    return jax.shard_map(
        on_device, mesh=mesh, in_specs=placed, out_specs=P("srv", ("grp", "kv")), check_vma=False
    )
```

```python
import functools
import math

import jax
import jax.numpy as jnp
from jax import lax
from jax.experimental import pallas as pl
from jax.experimental.pallas import tpu as pltpu
from jax.sharding import PartitionSpec as P

REACH = 4
EARLY = 3
FAR = -1e30
LAG = 5
MESH = pl.DeviceIdType.MESH


def layer(plan, lengths_in, q_hbm, k_hbm, v_hbm, w_ref, out_ref,
          lengths, q_in, k_in, v_in, q_ref, kv_ref, kvw, qbuf, bias, abuf, wbuf, acc,
          send1, recv1, send2, recv2, send3, recv3, far3, send4,
          ky_s, ky_r, kz_s, kz_r, sw_s, sw_r, q_s, q_r, own_w, w_s, w_r, a_s, a_r,
          s1, r1, s2, r2, s3, r3, s4, r4, in_s):
    head, heads, kvh, hp, hpp, halves, lanes, pairs, cw = plan
    tokens = q_ref.shape[0]
    inner = hp * head
    width = kvh * head
    split_kv = kv_ref.shape[2] > width
    own_chunks = w_ref.shape[1] // cw
    chunks = own_chunks * pairs
    items = lanes * pairs * chunks
    soon = own_chunks // 2
    segments = [(0, 2, 0, own_chunks), (0, 2, own_chunks, soon), (2, 1, 0, own_chunks + soon),
                (0, EARLY, own_chunks + soon, own_chunks - soon),
                (EARLY, lanes - EARLY, 0, chunks)]
    starts = [0]
    for _, planes, _, some in segments:
        starts.append(starts[-1] + planes * pairs * some)
    places = {}
    for (k0, planes, c0, some), n0 in zip(segments[:-1], starts):
        for r in range(planes * pairs * some):
            places[k0 + r // (pairs * some), r // some % pairs, c0 + r % some] = n0 + r
    swapped = (lanes - EARLY) * pairs * chunks
    ordered = [c for c in range(chunks) if c % own_chunks >= soon]
    ordered = ordered + [c for c in range(chunks) if c not in ordered]
    partner = [(c + own_chunks) % chunks for c in ordered]
    last = [[(k, c) for k in range(EARLY) for c in range(chunks) if (c % own_chunks < soon) == kind]
            for kind in (True, False)]
    settle = [
        max([max(places[k, 1, c], places[k, 0, (c + own_chunks) % chunks]) + LAG + 1 - m
             for m, (k, c) in enumerate(some)] + [starts[3] + 2])
        for some in last
    ]
    settle.append(settle[1] + swapped)
    settle[1] = max(settle[1], settle[0] + len(last[0]))
    settle[2] = max(settle[2], settle[0] + len(last[0]))
    back = REACH // pairs
    pieces = hp // hpp * pairs
    piece = hpp * head
    per_kv = hp // kvh
    per_run = per_kv // hpp
    each = -(-pieces // 3)
    wait_for = own_chunks * pairs - 1
    part = tokens // lanes
    a, g, s = lax.axis_index("grp"), lax.axis_index("kv"), lax.axis_index("srv")
    u, v = s // pairs, s % pairs
    q = a * halves + g
    ov = 1 - v

    core = (1 - a, g, s)
    beside = (a, g, u * pairs + ov)
    ahead = (a, g, s + pairs)
    behind = (a, g, s - pairs)
    right, left = u + 1 < lanes, u > 0
    at_home = q == u

    def other_half(k):
        return (a, (g + k) % halves, s)

    def owner(p):
        return (u // halves, u % halves, p * pairs + v)

    def giver(p):
        return (p // halves, p % halves, q * pairs + v)

    arriving = [
        pltpu.make_async_copy(src, dst, in_s.at[i])
        for i, (src, dst) in enumerate(
            ((k_hbm, k_in), (v_hbm, v_in), (q_hbm, q_in), (lengths_in, lengths)))
    ]
    for copy in arriving:
        copy.start()

    barrier = pltpu.get_barrier_semaphore()

    def greet(device):
        pl.semaphore_signal(barrier, inc=1, device_id=device, device_id_type=MESH)

    greet(core)
    greet(beside)
    for k in range(1, halves):
        greet(other_half(k))
    pl.when(right)(lambda: greet(ahead))
    pl.when(left)(lambda: greet(behind))
    for p in range(lanes):
        pl.when(jnp.logical_not(at_home & (q == p)))(lambda p=p: greet(giver(p)))
    peers = jnp.int32(1 + halves + lanes)
    peers = peers + jnp.where(right, 1, 0) + jnp.where(left, 1, 0) - jnp.where(at_home, 1, 0)

    def remote(src, dst, send, recv, device):
        return pltpu.make_async_remote_copy(
            src_ref=src, dst_ref=dst, send_sem=send, recv_sem=recv,
            device_id=device, device_id_type=MESH,
        )

    def lane_at(i, size):
        return pl.ds(pl.multiple_of(i, head), size)

    def kv_from(half, j):
        offset = half * width + j * head if split_kv else j * head
        return kv_ref.at[a, :, lane_at(offset, head)]

    def kv_at(m, back_by, w, j):
        return kvw.at[m, (back - back_by) * pairs + w, :, pl.ds(j * head, head)]

    def whose(w):
        return v if w == 0 else ov

    def kv_beside(j):
        return remote(kv_from(ov, j), kv_at(a, 0, v, j), ky_s.at[j], ky_r.at[j], beside)

    def kv_came(j):
        return remote(kv_from(ov, j), kv_at(a, 0, ov, j), ky_s.at[j], ky_r.at[j], beside)

    def kv_up(d, w, j):
        src = kv_from(v, j) if d == 1 and w == 0 else kv_at(a, d - 1, whose(w), j)
        return remote(src, kv_at(a, d, whose(w), j), kz_s.at[d - 1, w, j], kz_r.at[d - 1, w, j],
                      ahead)

    def swap(d, w, j, m):
        i = 0 if d == 0 else 2 * d - 1 + w
        ref = kv_at(m, d, whose(w), j)
        return remote(ref, ref, sw_s.at[i, j], sw_r.at[i, j], core)

    def query(j):
        size = per_kv * head
        return remote(q_ref.at[:, lane_at(ov * inner + j * size, size)],
                      qbuf.at[0, :, pl.ds(j * size, size)], q_s.at[j], q_r.at[j], beside)

    def weight(c):
        return remote(w_ref.at[pl.ds(ov * inner, inner), pl.ds(c * cw, cw)],
                      wbuf.at[own_chunks + c], w_s.at[c], w_r.at[c], beside)

    def own_weight(c):
        return pltpu.make_async_copy(
            w_ref.at[pl.ds(v * inner, inner), pl.ds(c * cw, cw)], wbuf.at[c], own_w.at[c])

    for c in range(own_chunks):
        own_weight(c).start()

    arriving[0].wait()
    arriving[1].wait()
    for j in range(k_in.shape[1]):
        kv_ref[0, :, j * head:(j + 1) * head] = k_in[:, j]
        kv_ref[1, :, j * head:(j + 1) * head] = v_in[:, j]

    pl.semaphore_wait(barrier, peers)

    for j in range(kvh):
        kv_beside(j).start()
        pl.when(right)(lambda j=j: kv_up(1, 0, j).start())
    span = q_in.shape[2]
    arriving[2].wait()
    for j in range(q_in.shape[1]):
        q_ref[:, j * span:(j + 1) * span] = q_in[:, j]
    for j in range(kvh):
        query(j).start()
    for c in range(own_chunks):
        weight(c).start()

    for m in range(2):
        offset = v * width if split_kv else 0
        kvw[m, back * pairs + v] = kv_ref[m, :, lane_at(offset, width)]
    qbuf[1] = q_ref[:, lane_at(v * inner, inner)]
    for d in range(1, back + 1):
        @pl.when(u < d)
        def _():
            for m in range(2):
                for w in range(pairs):
                    kvw[m, (back - d) * pairs + w] = jnp.zeros((tokens, width), kvw.dtype)

    arriving[3].wait()
    row = lax.broadcasted_iota(jnp.int32, (tokens, 1), 0)
    lane = lax.broadcasted_iota(jnp.int32, (tokens, tokens), 1)
    for h in range(pairs):
        shard = u * pairs + (ov if h == 0 else v)
        query_pos = shard * tokens + row
        first = jnp.zeros((tokens, 1), jnp.int32)
        start = jnp.int32(0)
        for i in range(lengths.shape[0]):
            first = jnp.where(query_pos >= start, start, first)
            start = start + lengths[i]
        for d in range(REACH + 1):
            key_pos = (shard - REACH + d) * tokens + lane
            allowed = (key_pos >= first) & (key_pos <= query_pos)
            bias[h, :, d * tokens:(d + 1) * tokens] = jnp.where(allowed, 0.0, FAR)

    def kv_hop(d, j):
        @pl.when(u >= d)
        def _():
            for w in range(pairs):
                kv_up(d, w, j).wait_recv()
                if d < back:
                    pl.when(right)(lambda w=w: kv_up(d + 1, w, j).start())
                swap(d, w, j, a).start()

    def kv_phase(j):
        kv_came(j).wait_recv()
        pl.when(right)(lambda: kv_up(1, 1, j).start())
        swap(0, 1, j, a).start()
        for d in range(1, back):
            kv_hop(d, j)

    def kv_ready(j):
        swap(0, 1, j, 1 - a).wait_recv()
        for d in range(1, back + 1):
            @pl.when(u >= d)
            def _():
                for w in range(pairs):
                    swap(d, w, j, 1 - a).wait_recv()

    def run(b):
        return b // kvh, b % kvh

    def bit(p, i):
        h, j = run(i // per_run)
        r = j * per_run + i % per_run
        return abuf.at[p, jnp.where(h == 0, ov, v), :, lane_at(r * piece, piece)]

    def relay(way, d, i):
        p = u - (d - 1) if way == 0 else u + (d - 1)
        return remote(bit(p, i), bit(p, i), a_s.at[way, d - 1], a_r.at[way, d - 1, i],
                      ahead if way == 0 else behind)

    def relayed(way, d, i):
        p = u - d if way == 0 else u + d
        return remote(bit(p, i), bit(p, i), a_s.at[way, d - 1], a_r.at[way, d - 1, i],
                      behind if way == 0 else ahead)

    def holds(way, d):
        return u >= d if way == 0 else u + d < lanes

    def may_send(way):
        return right if way == 0 else left

    def forward(d, i):
        for way in range(2):
            @pl.when(holds(way, d - 1) & may_send(way))
            def _():
                relayed(way, d - 1, i).wait_recv()
                relay(way, d, i).start()

    factor = math.log2(math.e) / math.sqrt(head)
    for j in range(min(2, kvh)):
        kv_phase(j)
    kv_hop(back, 0)
    kv_ready(0)

    def per_unit(i):
        h, kj = run(i // per_kv)
        hh = kj * per_kv + i % per_kv
        vv = jnp.where(h == 0, ov, v)
        for j in range(kvh):
            if j > 0:
                if j > 1:
                    pl.when(i == (j - 1) * per_kv)(lambda: kv_phase(j))
                pl.when(i == j * per_kv - 1)(lambda: kv_hop(back, j))
                pl.when(i == j * per_kv)(lambda: kv_ready(j))
            pl.when(i == j * per_kv)(lambda: query(j).wait_recv())
        mine = lane_at(hh * head, head)
        at = lane_at(kj * head, head)
        window = kvw[0, pl.ds(vv, REACH + 1), :, at].reshape((REACH + 1) * tokens, head)
        scores = lax.dot_general(
            qbuf[h, :, mine], window, (((1,), (1,)), ((), ())),
            preferred_element_type=jnp.float32,
        ) + bias[h]
        peak = jnp.max(scores, axis=1, keepdims=True)
        weights = jnp.exp2((scores - peak) * factor)
        total = jnp.sum(weights, axis=1, keepdims=True)
        numer = jnp.dot(
            weights.astype(jnp.bfloat16),
            kvw[1, pl.ds(vv, REACH + 1), :, at].reshape((REACH + 1) * tokens, head),
            preferred_element_type=jnp.float32,
        )
        abuf[u, vv, :, mine] = (numer / total).astype(abuf.dtype)

        @pl.when(i % hpp == hpp - 1)
        def _():
            n = i // hpp
            for way in range(2):
                pl.when(may_send(way))(lambda: relay(way, 1, n).start())

    units = hp * pairs
    ahead_by = units - own_chunks - 1

    def plane(k):
        low = jnp.minimum(u, lanes - 1 - u)
        zigzag = jnp.where(k % 2 == 1, u - (k + 1) // 2, u + k // 2)
        line = jnp.where(u < lanes - 1 - u, k, lanes - 1 - k)
        return jnp.where(k <= 2 * low, zigzag, line)

    inside = left & right

    def pick(i, values):
        found = jnp.int32(values[0])
        for at, value in enumerate(values[1:], 1):
            found = jnp.where(i == at, value, found)
        return found

    def decode(n):
        k, h, c = jnp.int32(0), jnp.int32(0), jnp.int32(0)
        fresh = jnp.bool_(False)
        kept_in = n < items
        m = jnp.where(n < starts[3] + swapped, n + starts[4] - starts[3], n - swapped)
        n = jnp.where(inside & (n >= starts[3]) & (n < items), m, n)
        for (k0, planes, c0, some), n0 in zip(segments, starts):
            if planes * some == 0:
                continue
            r = n - n0
            here = r >= 0
            half, order = r // some % pairs, c0 + r % some
            if k0 == EARLY:
                order = jnp.where(half == 0, pick(r % some, ordered), pick(r % some, partner))
            k = jnp.where(here, k0 + r // (pairs * some), k)
            h = jnp.where(here, half, h)
            c = jnp.where(here, order, c)
            fresh = jnp.where(here, (r % some == 0) & (c0 == 0), fresh)
        return k, h, c, fresh & (k > 0) & kept_in

    def column(c):
        return jnp.where(c < own_chunks, v * own_chunks + c, ov * own_chunks + c - own_chunks)

    def to_core(n):
        return remote(send1.at[n], recv1.at[n], s1.at[0], r1.at[n], core)

    def to_half(n, k):
        rows = pl.ds((g + k) % halves * part, part)
        return remote(send2.at[n, rows], recv2.at[n, k - 1], s2.at[0], r2.at[n], other_half(k))

    def all_halves(n):
        return remote(recv2.at[n], recv2.at[n], s2.at[0], r2.at[n], other_half(1))

    def to_beside(k, c):
        i = k * chunks + c
        return remote(send3.at[i], recv3.at[i], s3.at[0], r3.at[i], beside)

    def result(giver_index, c):
        return out_ref.at[pl.ds(giver_index * part, part), lane_at(c * cw, cw)]

    def to_owner(k, c):
        return remote(send4.at[k * chunks + c], result(q, c), s4.at[0], r4.at[0], owner(plane(k)))

    def to_self(c):
        return pltpu.make_async_copy(send4.at[c], result(q, c), r4.at[0])

    def stage1(n):
        k, h, c, _ = decode(n)
        product = jnp.dot(abuf[plane(k), jnp.where(h == 0, ov, v)], wbuf[c],
                          preferred_element_type=jnp.float32)
        low, high = product[:tokens // 2], product[tokens // 2:]
        acc[n] = jnp.where(a == 0, low, high)
        send1[n] = jnp.where(a == 0, high, low).astype(send1.dtype)
        to_core(n).start()

    def far_beside(k, c, n):
        return remote(send2.at[n], far3.at[(k - EARLY) * chunks + c], s3.at[1],
                      r3.at[k * chunks + c], beside)

    def to_halves(n, total):
        acc[n] = total
        send2[n] = total.astype(send2.dtype)
        for k in range(1, halves):
            to_half(n, k).start()

    def direct(k, c):
        return (k >= EARLY) & (c % own_chunks >= soon)

    def stage2(n):
        k, h, c, _ = decode(n)
        col = column(c)
        to_core(n).wait_recv()
        total = acc[n] + recv1[n].astype(jnp.float32)
        y_first = direct(k, c)
        pl.when(jnp.logical_not(y_first))(lambda: to_halves(n, total))

        @pl.when(y_first & (h == 0))
        def _():
            send2[n] = total.astype(send2.dtype)
            far_beside(k, col, n).start()

        @pl.when(y_first & (h != 0))
        def _():
            far_beside(k, col, n).wait_recv()
            to_halves(n, total + far3[(k - EARLY) * chunks + col].astype(jnp.float32))

    kept = pl.ds(g * part, part)

    def deliver(k, col, total):
        send4[k * chunks + col] = total.astype(send4.dtype)
        pl.when(at_home & (k == 0))(lambda: to_self(col).start())
        pl.when(jnp.logical_not(at_home & (k == 0)))(lambda: to_owner(k, col).start())

    def stage3(n):
        k, h, c, _ = decode(n)
        col = column(c)

        y_first = direct(k, c)

        @pl.when(jnp.logical_not(y_first) | (h != 0))
        def _():
            all_halves(n).wait_recv()
            total = acc[n, kept]
            for i in range(halves - 1):
                total = total + recv2[n, i].astype(jnp.float32)

            @pl.when(h == 0)
            def _():
                send3[k * chunks + col] = total.astype(send3.dtype)
                to_beside(k, col).start()

            @pl.when((h != 0) & (k < EARLY))
            def _():
                acc[n, kept] = total

            pl.when((h != 0) & y_first)(lambda: deliver(k, col, total))

            @pl.when((h != 0) & (k >= EARLY) & jnp.logical_not(y_first))
            def _():
                to_beside(k, col).wait_recv()
                deliver(k, col, total + recv3[k * chunks + col].astype(jnp.float32))

    def stage4(n, k, c):
        col = column(c)
        to_beside(k, col).wait_recv()
        deliver(k, col, acc[n, kept] + recv3[k * chunks + col].astype(jnp.float32))

    def arrived(k, h):
        p = plane(k)
        up = p < u
        d = jnp.where(up, u - p, p - u)
        way = jnp.where(up, 0, 1)

        @pl.when(jnp.logical_not(jnp.where(up, right, left)))
        def _():
            def one(r, carry):
                i = h * kvh * per_run + r
                remote(bit(p, i), bit(p, i), a_s.at[way, d - 1], a_r.at[way, d - 1, i],
                       core).wait_recv()
                return carry

            lax.fori_loop(0, kvh * per_run, one, 0)

    def per_item(n):
        k, h, c, fresh = decode(n)

        f = (n - wait_for) * each

        @pl.when((f >= 0) & (f < pieces))
        def _():
            for i in range(each):
                pl.when(f + i < pieces)(lambda i=i: forward(2, f + i))

        if lanes > 3:
            for i in range(pieces):
                at = starts[1] + (starts[3] - starts[1] + 1) * i // pieces
                pl.when(n == at)(lambda i=i: forward(3, i))
        if lanes > 4:
            @pl.when(n == starts[3])
            def _():
                for d in range(4, lanes):
                    def one(i, carry):
                        forward(d, i)
                        return carry

                    lax.fori_loop(0, pieces, one, 0)

        for i in range(own_chunks):
            used = starts[1] + i if i < soon else starts[3]
            pl.when(n == used)(lambda i=i: weight(i).wait_recv())
        done = decode(n - 1)[3]
        pl.when(fresh & jnp.logical_not(done) & (n >= 2))(lambda: stage2(n - 2))

        @pl.when(fresh)
        def _():
            stage2(n - 1)
            arrived(k, h)

        pl.when(n < items)(lambda: stage1(n))
        pending = jnp.logical_not(fresh | done) & (n >= 2 + own_chunks) & (n < items + 2)
        pl.when(pending)(lambda: stage2(n - 2))
        pl.when((n >= LAG) & (n < items + LAG))(lambda: stage3(n - LAG))
        later = jnp.where(inside, swapped, 0)
        index, mk, mc = jnp.int32(-1), jnp.int32(0), jnp.int32(0)
        begins = settle[0], jnp.where(inside, settle[2], settle[1])
        for some, first, shift in zip(last, begins, (0, later)):
            for m, (k1, c1) in enumerate(some):
                here = n == first + m
                held = places[k1, 1, c1]
                index = jnp.where(here, held + (shift if held >= starts[3] else 0), index)
                mk, mc = jnp.where(here, k1, mk), jnp.where(here, c1, mc)
        pl.when(index >= 0)(lambda: stage4(index, mk, mc))

    def step(i, carry):
        pl.when(i < units)(lambda: per_unit(i))
        for c in range(own_chunks):
            @pl.when(i == hp + 2 * c)
            def _():
                own_weight(c).wait()
                stage1(c)

            pl.when(i == hp + 2 * c + 1)(lambda: stage2(c))
        pl.when(i >= units - 1)(lambda: per_item(i - ahead_by))
        return carry

    lax.fori_loop(0, ahead_by + max(items + LAG, settle[2] + len(last[1])), step, 0)

    far = (lanes - EARLY) * sum(c % own_chunks >= soon for c in range(chunks))

    def sent(ref, sem):
        remote(ref, ref, sem, sem, core).wait_send()

    for j in range(kvh):
        kv_beside(j).wait_send()
        query(j).wait_send()
        swap(0, 1, j, a).wait_send()
        for d in range(1, back + 1):
            for w in range(pairs):
                pl.when((u >= d - 1) & right)(lambda d=d, w=w, j=j: kv_up(d, w, j).wait_send())
                pl.when(u >= d)(lambda d=d, w=w, j=j: swap(d, w, j, a).wait_send())
    for c in range(own_chunks):
        weight(c).wait_send()
    for d in range(1, lanes):
        for way in range(2):
            p = u - (d - 1) if way == 0 else u + (d - 1)
            pl.when(holds(way, d - 1) & may_send(way))(
                lambda p=p, way=way, d=d: sent(abuf.at[p], a_s.at[way, d - 1]))

    sent(send1, s1.at[0])
    sent(recv2.at[pl.ds(0, items - far)], s2.at[0])
    sent(send3.at[pl.ds(0, lanes * chunks - far)], s3.at[0])
    sent(far3.at[pl.ds(0, far)], s3.at[1])
    pl.when(at_home)(lambda: sent(send4.at[pl.ds(chunks, (lanes - 1) * chunks)], s4.at[0]))
    pl.when(jnp.logical_not(at_home))(lambda: sent(send4, s4.at[0]))
    pltpu.make_async_copy(out_ref, out_ref, r4.at[0]).wait()


def on_device(queries, keys, values, lengths, output_projection_weight):
    tokens = queries.shape[0]
    cores, halves = lax.axis_size("grp"), lax.axis_size("kv")
    lanes = cores * halves
    pairs = lax.axis_size("srv") // lanes
    assert cores == 2 and pairs == 2 and halves > 1 and lanes > EARLY
    groups, head = keys.shape[1], keys.shape[2]
    inner = groups * queries.shape[2]
    weight = output_projection_weight.reshape(inner, -1)
    columns = weight.shape[1]
    heads = inner // (groups * head)
    kvh = max(1, groups // pairs)
    hp = inner // head // pairs
    hpp = 2
    cw = max(256, columns // 2)
    own_chunks = columns // cw
    chunks = own_chunks * pairs
    items = lanes * pairs * chunks
    pieces = hp // hpp * pairs
    part = tokens // lanes
    back = REACH // pairs
    width = kvh * head
    dma = pltpu.SemaphoreType.DMA
    bf16, f32 = jnp.bfloat16, jnp.float32
    hbm = pl.BlockSpec(memory_space=pltpu.HBM)
    return pl.pallas_call(
        functools.partial(layer, (head, heads, kvh, hp, hpp, halves, lanes, pairs, cw)),
        out_shape=jax.ShapeDtypeStruct((tokens, pairs * columns), bf16),
        in_specs=[hbm] * 5,
        out_specs=pl.BlockSpec(memory_space=pl.ANY),
        scratch_shapes=[
            pltpu.SMEM(lengths.shape, lengths.dtype),
            pltpu.VMEM(queries.shape, bf16),
            pltpu.VMEM(keys.shape, bf16),
            pltpu.VMEM(values.shape, bf16),
            pltpu.VMEM((tokens, inner), bf16),
            pltpu.VMEM((2, tokens, groups * head), bf16),
            pltpu.VMEM((2, (back + 1) * pairs, tokens, width), bf16),
            pltpu.VMEM((pairs, tokens, hp * head), bf16),
            pltpu.VMEM((pairs, tokens, (REACH + 1) * tokens), f32),
            pltpu.VMEM((lanes, pairs, tokens, hp * head), bf16),
            pltpu.VMEM((chunks, hp * head, cw), bf16),
            pltpu.VMEM((items, tokens // cores, cw), f32),
            pltpu.VMEM((items, tokens // cores, cw), bf16),
            pltpu.VMEM((items, tokens // cores, cw), bf16),
            pltpu.VMEM((items, tokens // cores, cw), bf16),
            pltpu.VMEM((items, halves - 1, part, cw), bf16),
            pltpu.VMEM((lanes * chunks, part, cw), bf16),
            pltpu.VMEM((lanes * chunks, part, cw), bf16),
            pltpu.VMEM(((lanes - EARLY) * chunks, tokens // cores, cw), bf16),
            pltpu.VMEM((lanes * chunks, part, cw), bf16),
            dma((kvh,)), dma((kvh,)), dma((back, pairs, kvh)), dma((back, pairs, kvh)),
            dma((2 * back + 1, kvh)), dma((2 * back + 1, kvh)), dma((kvh,)), dma((kvh,)),
            dma((own_chunks,)), dma((own_chunks,)), dma((own_chunks,)),
            dma((2, lanes - 1)), dma((2, lanes - 1, pieces)),
            dma((1,)), dma((items,)), dma((1,)), dma((items,)),
            dma((2,)), dma((lanes * chunks,)), dma((1,)), dma((1,)),
            dma((4,)),
        ],
        compiler_params=pltpu.CompilerParams(
            collective_id=0, has_side_effects=True, vmem_limit_bytes=52 * 1024 * 1024
        ),
    )(*[pltpu.with_memory_space_constraint(x, pltpu.HBM) for x in (lengths, queries, keys, values, weight)])


def solution(mesh):
    placed = (
        P("srv", "kv", "grp"),
        P("srv", "kv", None),
        P("srv", "kv", None),
        P(),
        P("kv", "grp", "srv"),
    )
    return jax.shard_map(
        on_device, mesh=mesh, in_specs=placed, out_specs=P("srv", ("grp", "kv")), check_vma=False
    )
```

```python
import functools
import math

import jax
import jax.numpy as jnp
from jax import lax
from jax.experimental import pallas as pl
from jax.experimental.pallas import tpu as pltpu
from jax.sharding import PartitionSpec as P

REACH = 4
EARLY = 3
FAR = -1e30
LAG = 5
RING = 8
MESH = pl.DeviceIdType.MESH


def layer(plan, lengths_in, q_hbm, k_hbm, v_hbm, w_ref, out_ref,
          lengths, q_in, k_in, v_in, q_ref, kv_ref, kvw, qbuf, bias, abuf, wbuf, acc,
          send1, recv1, send2, recv2, send3, recv3, far3, send4,
          ky_s, ky_r, kz_s, kz_r, sw_s, sw_r, q_s, q_r, own_w, w_s, w_r, a_s, a_r,
          s1, r1, s2, r2, s3, r3, s4, r4, in_s):
    head, heads, kvh, hp, hpp, halves, lanes, pairs, cw = plan
    tokens = q_ref.shape[0]
    inner = hp * head
    width = kvh * head
    split_kv = kv_ref.shape[2] > width
    own_chunks = w_ref.shape[1] // cw
    chunks = own_chunks * pairs
    items = lanes * pairs * chunks
    soon = own_chunks // 2
    segments = [(0, 2, 0, own_chunks), (0, 2, own_chunks, soon), (2, 1, 0, own_chunks + soon),
                (0, EARLY, own_chunks + soon, own_chunks - soon),
                (EARLY, lanes - EARLY, 0, chunks)]
    starts = [0]
    for _, planes, _, some in segments:
        starts.append(starts[-1] + planes * pairs * some)
    places = {}
    for (k0, planes, c0, some), n0 in zip(segments[:-1], starts):
        for r in range(planes * pairs * some):
            places[k0 + r // (pairs * some), r // some % pairs, c0 + r % some] = n0 + r
    swapped = (lanes - EARLY) * pairs * chunks
    ordered = [c for c in range(chunks) if c % own_chunks >= soon]
    ordered = ordered + [c for c in range(chunks) if c not in ordered]
    partner = [(c + own_chunks) % chunks for c in ordered]
    last = [[(k, c) for k in range(EARLY) for c in range(chunks) if (c % own_chunks < soon) == kind]
            for kind in (True, False)]
    settle = [
        max([max(places[k, 1, c], places[k, 0, (c + own_chunks) % chunks]) + LAG + 1 - m
             for m, (k, c) in enumerate(some)] + [starts[3] + 2])
        for some in last
    ]
    settle.append(settle[1] + swapped)
    settle[1] = max(settle[1], settle[0] + len(last[0]))
    settle[2] = max(settle[2], settle[0] + len(last[0]))
    back = REACH // pairs
    pieces = hp // hpp * pairs
    piece = hpp * head
    per_kv = hp // kvh
    per_run = per_kv // hpp
    each = -(-pieces // 3)
    wait_for = own_chunks * pairs - 1
    part = tokens // lanes
    a, g, s = lax.axis_index("grp"), lax.axis_index("kv"), lax.axis_index("srv")
    u, v = s // pairs, s % pairs
    q = a * halves + g
    ov = 1 - v

    core = (1 - a, g, s)
    beside = (a, g, u * pairs + ov)
    ahead = (a, g, s + pairs)
    behind = (a, g, s - pairs)
    right, left = u + 1 < lanes, u > 0
    at_home = q == u

    def other_half(k):
        return (a, (g + k) % halves, s)

    def owner(p):
        return (u // halves, u % halves, p * pairs + v)

    def giver(p):
        return (p // halves, p % halves, q * pairs + v)

    arriving = [
        pltpu.make_async_copy(src, dst, in_s.at[i])
        for i, (src, dst) in enumerate(
            ((k_hbm, k_in), (v_hbm, v_in), (q_hbm, q_in), (lengths_in, lengths)))
    ]
    for copy in arriving:
        copy.start()

    barrier = pltpu.get_barrier_semaphore()

    def greet(device):
        pl.semaphore_signal(barrier, inc=1, device_id=device, device_id_type=MESH)

    greet(core)
    greet(beside)
    for k in range(1, halves):
        greet(other_half(k))
    pl.when(right)(lambda: greet(ahead))
    pl.when(left)(lambda: greet(behind))
    for p in range(lanes):
        pl.when(jnp.logical_not(at_home & (q == p)))(lambda p=p: greet(giver(p)))
    peers = jnp.int32(1 + halves + lanes)
    peers = peers + jnp.where(right, 1, 0) + jnp.where(left, 1, 0) - jnp.where(at_home, 1, 0)

    def remote(src, dst, send, recv, device):
        return pltpu.make_async_remote_copy(
            src_ref=src, dst_ref=dst, send_sem=send, recv_sem=recv,
            device_id=device, device_id_type=MESH,
        )

    def lane_at(i, size):
        return pl.ds(pl.multiple_of(i, head), size)

    def kv_from(half, j):
        offset = half * width + j * head if split_kv else j * head
        return kv_ref.at[a, :, lane_at(offset, head)]

    def kv_at(m, back_by, w, j):
        return kvw.at[m, (back - back_by) * pairs + w, :, pl.ds(j * head, head)]

    def whose(w):
        return v if w == 0 else ov

    def kv_beside(j):
        return remote(kv_from(ov, j), kv_at(a, 0, v, j), ky_s.at[j], ky_r.at[j], beside)

    def kv_came(j):
        return remote(kv_from(ov, j), kv_at(a, 0, ov, j), ky_s.at[j], ky_r.at[j], beside)

    def kv_up(d, w, j):
        src = kv_from(v, j) if d == 1 and w == 0 else kv_at(a, d - 1, whose(w), j)
        return remote(src, kv_at(a, d, whose(w), j), kz_s.at[d - 1, w, j], kz_r.at[d - 1, w, j],
                      ahead)

    def swap(d, w, j, m):
        i = 0 if d == 0 else 2 * d - 1 + w
        ref = kv_at(m, d, whose(w), j)
        return remote(ref, ref, sw_s.at[i, j], sw_r.at[i, j], core)

    def query(j):
        size = per_kv * head
        return remote(q_ref.at[:, lane_at(ov * inner + j * size, size)],
                      qbuf.at[0, :, pl.ds(j * size, size)], q_s.at[j], q_r.at[j], beside)

    def weight(c):
        return remote(w_ref.at[pl.ds(ov * inner, inner), pl.ds(c * cw, cw)],
                      wbuf.at[own_chunks + c], w_s.at[c], w_r.at[c], beside)

    def own_weight(c):
        return pltpu.make_async_copy(
            w_ref.at[pl.ds(v * inner, inner), pl.ds(c * cw, cw)], wbuf.at[c], own_w.at[c])

    for c in range(own_chunks):
        own_weight(c).start()

    arriving[0].wait()
    arriving[1].wait()
    for j in range(k_in.shape[1]):
        kv_ref[0, :, j * head:(j + 1) * head] = k_in[:, j]
        kv_ref[1, :, j * head:(j + 1) * head] = v_in[:, j]

    pl.semaphore_wait(barrier, peers)

    for j in range(kvh):
        kv_beside(j).start()
        pl.when(right)(lambda j=j: kv_up(1, 0, j).start())
    span = q_in.shape[2]
    arriving[2].wait()
    for j in range(q_in.shape[1]):
        q_ref[:, j * span:(j + 1) * span] = q_in[:, j]
    for j in range(kvh):
        query(j).start()
    for c in range(own_chunks):
        weight(c).start()

    for m in range(2):
        offset = v * width if split_kv else 0
        kvw[m, back * pairs + v] = kv_ref[m, :, lane_at(offset, width)]
    qbuf[1] = q_ref[:, lane_at(v * inner, inner)]
    for d in range(1, back + 1):
        @pl.when(u < d)
        def _():
            for m in range(2):
                for w in range(pairs):
                    kvw[m, (back - d) * pairs + w] = jnp.zeros((tokens, width), kvw.dtype)

    arriving[3].wait()
    row = lax.broadcasted_iota(jnp.int32, (tokens, 1), 0)
    lane = lax.broadcasted_iota(jnp.int32, (tokens, tokens), 1)
    for h in range(pairs):
        shard = u * pairs + (ov if h == 0 else v)
        query_pos = shard * tokens + row
        first = jnp.zeros((tokens, 1), jnp.int32)
        start = jnp.int32(0)
        for i in range(lengths.shape[0]):
            first = jnp.where(query_pos >= start, start, first)
            start = start + lengths[i]
        for d in range(REACH + 1):
            key_pos = (shard - REACH + d) * tokens + lane
            allowed = (key_pos >= first) & (key_pos <= query_pos)
            bias[h, :, d * tokens:(d + 1) * tokens] = jnp.where(allowed, 0.0, FAR)

    def kv_hop(d, j):
        @pl.when(u >= d)
        def _():
            for w in range(pairs):
                kv_up(d, w, j).wait_recv()
                if d < back:
                    pl.when(right)(lambda w=w: kv_up(d + 1, w, j).start())
                swap(d, w, j, a).start()

    def kv_phase(j):
        kv_came(j).wait_recv()
        pl.when(right)(lambda: kv_up(1, 1, j).start())
        swap(0, 1, j, a).start()
        for d in range(1, back):
            kv_hop(d, j)

    def kv_ready(j):
        swap(0, 1, j, 1 - a).wait_recv()
        for d in range(1, back + 1):
            @pl.when(u >= d)
            def _():
                for w in range(pairs):
                    swap(d, w, j, 1 - a).wait_recv()

    def run(b):
        return b // kvh, b % kvh

    def bit(p, i):
        h, j = run(i // per_run)
        r = j * per_run + i % per_run
        return abuf.at[p, jnp.where(h == 0, ov, v), :, lane_at(r * piece, piece)]

    def relay(way, d, i):
        p = u - (d - 1) if way == 0 else u + (d - 1)
        return remote(bit(p, i), bit(p, i), a_s.at[way, d - 1], a_r.at[way, d - 1, i],
                      ahead if way == 0 else behind)

    def relayed(way, d, i):
        p = u - d if way == 0 else u + d
        return remote(bit(p, i), bit(p, i), a_s.at[way, d - 1], a_r.at[way, d - 1, i],
                      behind if way == 0 else ahead)

    def holds(way, d):
        return u >= d if way == 0 else u + d < lanes

    def may_send(way):
        return right if way == 0 else left

    def forward(d, i):
        for way in range(2):
            @pl.when(holds(way, d - 1) & may_send(way))
            def _():
                relayed(way, d - 1, i).wait_recv()
                relay(way, d, i).start()

    factor = math.log2(math.e) / math.sqrt(head)
    for j in range(min(2, kvh)):
        kv_phase(j)
    kv_hop(back, 0)
    kv_ready(0)

    def per_unit(i):
        h, kj = run(i // per_kv)
        hh = kj * per_kv + i % per_kv
        vv = jnp.where(h == 0, ov, v)
        for j in range(kvh):
            if j > 0:
                if j > 1:
                    pl.when(i == (j - 1) * per_kv)(lambda: kv_phase(j))
                pl.when(i == j * per_kv - 1)(lambda: kv_hop(back, j))
                pl.when(i == j * per_kv)(lambda: kv_ready(j))
            pl.when(i == j * per_kv)(lambda: query(j).wait_recv())
        mine = lane_at(hh * head, head)
        at = lane_at(kj * head, head)
        window = kvw[0, pl.ds(vv, REACH + 1), :, at].reshape((REACH + 1) * tokens, head)
        scores = lax.dot_general(
            qbuf[h, :, mine], window, (((1,), (1,)), ((), ())),
            preferred_element_type=jnp.float32,
        ) + bias[h]
        peak = jnp.max(scores, axis=1, keepdims=True)
        weights = jnp.exp2((scores - peak) * factor)
        total = jnp.sum(weights, axis=1, keepdims=True)
        numer = jnp.dot(
            weights.astype(jnp.bfloat16),
            kvw[1, pl.ds(vv, REACH + 1), :, at].reshape((REACH + 1) * tokens, head),
            preferred_element_type=jnp.float32,
        )
        abuf[u, vv, :, mine] = (numer / total).astype(abuf.dtype)

        @pl.when(i % hpp == hpp - 1)
        def _():
            n = i // hpp
            for way in range(2):
                pl.when(may_send(way))(lambda: relay(way, 1, n).start())

    units = hp * pairs
    ahead_by = units - own_chunks - 1

    def plane(k):
        low = jnp.minimum(u, lanes - 1 - u)
        zigzag = jnp.where(k % 2 == 1, u - (k + 1) // 2, u + k // 2)
        line = jnp.where(u < lanes - 1 - u, k, lanes - 1 - k)
        return jnp.where(k <= 2 * low, zigzag, line)

    inside = left & right

    def pick(i, values):
        found = jnp.int32(values[0])
        for at, value in enumerate(values[1:], 1):
            found = jnp.where(i == at, value, found)
        return found

    def decode(n):
        k, h, c = jnp.int32(0), jnp.int32(0), jnp.int32(0)
        fresh = jnp.bool_(False)
        kept_in = n < items
        m = jnp.where(n < starts[3] + swapped, n + starts[4] - starts[3], n - swapped)
        n = jnp.where(inside & (n >= starts[3]) & (n < items), m, n)
        for (k0, planes, c0, some), n0 in zip(segments, starts):
            if planes * some == 0:
                continue
            r = n - n0
            here = r >= 0
            half, order = r // some % pairs, c0 + r % some
            if k0 == EARLY:
                order = jnp.where(half == 0, pick(r % some, ordered), pick(r % some, partner))
            k = jnp.where(here, k0 + r // (pairs * some), k)
            h = jnp.where(here, half, h)
            c = jnp.where(here, order, c)
            fresh = jnp.where(here, (r % some == 0) & (c0 == 0), fresh)
        return k, h, c, fresh & (k > 0) & kept_in

    def column(c):
        return jnp.where(c < own_chunks, v * own_chunks + c, ov * own_chunks + c - own_chunks)

    def to_core(n):
        return remote(send1.at[n], recv1.at[n], s1.at[0], r1.at[n % RING], core)

    def to_half(n, k):
        rows = pl.ds((g + k) % halves * part, part)
        return remote(send2.at[n, rows], recv2.at[n, k - 1], s2.at[0], r2.at[n % (2 * RING)], other_half(k))

    def all_halves(n):
        return remote(recv2.at[n], recv2.at[n], s2.at[0], r2.at[n % (2 * RING)], other_half(1))

    def to_beside(k, c):
        i = k * chunks + c
        return remote(send3.at[i], recv3.at[i], s3.at[0], r3.at[i], beside)

    def result(giver_index, c):
        return out_ref.at[pl.ds(giver_index * part, part), lane_at(c * cw, cw)]

    def to_owner(k, c):
        return remote(send4.at[k * chunks + c], result(q, c), s4.at[0], r4.at[0], owner(plane(k)))

    def to_self(c):
        return pltpu.make_async_copy(send4.at[c], result(q, c), r4.at[0])

    def stage1(n):
        k, h, c, _ = decode(n)
        product = jnp.dot(abuf[plane(k), jnp.where(h == 0, ov, v)], wbuf[c],
                          preferred_element_type=jnp.float32)
        low, high = product[:tokens // 2], product[tokens // 2:]
        acc[n] = jnp.where(a == 0, low, high)
        send1[n] = jnp.where(a == 0, high, low).astype(send1.dtype)
        to_core(n).start()

    def far_beside(k, c, n):
        return remote(send2.at[n], far3.at[(k - EARLY) * chunks + c], s3.at[1],
                      r3.at[k * chunks + c], beside)

    def to_halves(n, total):
        acc[n] = total
        send2[n] = total.astype(send2.dtype)
        for k in range(1, halves):
            to_half(n, k).start()

    def direct(k, c):
        return k >= EARLY

    def stage2(n):
        k, h, c, _ = decode(n)
        col = column(c)
        to_core(n).wait_recv()
        total = acc[n] + recv1[n].astype(jnp.float32)
        y_first = direct(k, c)
        pl.when(jnp.logical_not(y_first))(lambda: to_halves(n, total))

        @pl.when(y_first & (h == 0))
        def _():
            send2[n] = total.astype(send2.dtype)
            far_beside(k, col, n).start()

        @pl.when(y_first & (h != 0))
        def _():
            far_beside(k, col, n).wait_recv()
            to_halves(n, total + far3[(k - EARLY) * chunks + col].astype(jnp.float32))

    kept = pl.ds(g * part, part)

    def deliver(k, col, total):
        send4[k * chunks + col] = total.astype(send4.dtype)
        pl.when(at_home & (k == 0))(lambda: to_self(col).start())
        pl.when(jnp.logical_not(at_home & (k == 0)))(lambda: to_owner(k, col).start())

    def stage3(n):
        k, h, c, _ = decode(n)
        col = column(c)

        y_first = direct(k, c)

        @pl.when(jnp.logical_not(y_first) | (h != 0))
        def _():
            all_halves(n).wait_recv()
            total = acc[n, kept]
            for i in range(halves - 1):
                total = total + recv2[n, i].astype(jnp.float32)

            @pl.when(h == 0)
            def _():
                send3[k * chunks + col] = total.astype(send3.dtype)
                to_beside(k, col).start()

            @pl.when((h != 0) & (k < EARLY))
            def _():
                acc[n, kept] = total

            pl.when((h != 0) & y_first)(lambda: deliver(k, col, total))

            @pl.when((h != 0) & (k >= EARLY) & jnp.logical_not(y_first))
            def _():
                to_beside(k, col).wait_recv()
                deliver(k, col, total + recv3[k * chunks + col].astype(jnp.float32))

    def stage4(n, k, c):
        col = column(c)
        to_beside(k, col).wait_recv()
        deliver(k, col, acc[n, kept] + recv3[k * chunks + col].astype(jnp.float32))

    def arrived(k, h):
        p = plane(k)
        up = p < u
        d = jnp.where(up, u - p, p - u)
        way = jnp.where(up, 0, 1)

        @pl.when(jnp.logical_not(jnp.where(up, right, left)))
        def _():
            def one(r, carry):
                i = h * kvh * per_run + r
                remote(bit(p, i), bit(p, i), a_s.at[way, d - 1], a_r.at[way, d - 1, i],
                       core).wait_recv()
                return carry

            lax.fori_loop(0, kvh * per_run, one, 0)

    def per_item(n):
        k, h, c, fresh = decode(n)

        f = (n - wait_for) * each

        @pl.when((f >= 0) & (f < pieces))
        def _():
            for i in range(each):
                pl.when(f + i < pieces)(lambda i=i: forward(2, f + i))

        if lanes > 3:
            for i in range(pieces):
                at = starts[1] + (starts[3] - starts[1] + 1) * i // pieces
                pl.when(n == at)(lambda i=i: forward(3, i))
        if lanes > 4:
            @pl.when(n == starts[3])
            def _():
                for d in range(4, lanes):
                    def one(i, carry):
                        forward(d, i)
                        return carry

                    lax.fori_loop(0, pieces, one, 0)

        for i in range(own_chunks):
            used = starts[1] + i if i < soon else starts[3]
            pl.when(n == used)(lambda i=i: weight(i).wait_recv())
        done = decode(n - 1)[3]
        pl.when(fresh & jnp.logical_not(done) & (n >= 2))(lambda: stage2(n - 2))

        @pl.when(fresh)
        def _():
            stage2(n - 1)
            arrived(k, h)

        pl.when(n < items)(lambda: stage1(n))
        pending = jnp.logical_not(fresh | done) & (n >= 2 + own_chunks) & (n < items + 2)
        pl.when(pending)(lambda: stage2(n - 2))
        pl.when((n >= LAG) & (n < items + LAG))(lambda: stage3(n - LAG))
        later = jnp.where(inside, swapped, 0)
        index, mk, mc = jnp.int32(-1), jnp.int32(0), jnp.int32(0)
        begins = settle[0], jnp.where(inside, settle[2], settle[1])
        for some, first, shift in zip(last, begins, (0, later)):
            for m, (k1, c1) in enumerate(some):
                here = n == first + m
                held = places[k1, 1, c1]
                index = jnp.where(here, held + (shift if held >= starts[3] else 0), index)
                mk, mc = jnp.where(here, k1, mk), jnp.where(here, c1, mc)
        pl.when(index >= 0)(lambda: stage4(index, mk, mc))

    def step(i, carry):
        pl.when(i < units)(lambda: per_unit(i))
        for c in range(own_chunks):
            @pl.when(i == hp + 2 * c)
            def _():
                own_weight(c).wait()
                stage1(c)

            pl.when(i == hp + 2 * c + 1)(lambda: stage2(c))
        pl.when(i >= units - 1)(lambda: per_item(i - ahead_by))
        return carry

    lax.fori_loop(0, ahead_by + max(items + LAG, settle[2] + len(last[1])), step, 0)

    far = (lanes - EARLY) * chunks

    def sent(ref, sem):
        remote(ref, ref, sem, sem, core).wait_send()

    for j in range(kvh):
        kv_beside(j).wait_send()
        query(j).wait_send()
        swap(0, 1, j, a).wait_send()
        for d in range(1, back + 1):
            for w in range(pairs):
                pl.when((u >= d - 1) & right)(lambda d=d, w=w, j=j: kv_up(d, w, j).wait_send())
                pl.when(u >= d)(lambda d=d, w=w, j=j: swap(d, w, j, a).wait_send())
    for c in range(own_chunks):
        weight(c).wait_send()
    for d in range(1, lanes):
        for way in range(2):
            p = u - (d - 1) if way == 0 else u + (d - 1)
            pl.when(holds(way, d - 1) & may_send(way))(
                lambda p=p, way=way, d=d: sent(abuf.at[p], a_s.at[way, d - 1]))

    sent(send1, s1.at[0])
    sent(recv2.at[pl.ds(0, items - far)], s2.at[0])
    sent(send3.at[pl.ds(0, lanes * chunks - far)], s3.at[0])
    sent(far3.at[pl.ds(0, far)], s3.at[1])
    pl.when(at_home)(lambda: sent(send4.at[pl.ds(chunks, (lanes - 1) * chunks)], s4.at[0]))
    pl.when(jnp.logical_not(at_home))(lambda: sent(send4, s4.at[0]))
    pltpu.make_async_copy(out_ref, out_ref, r4.at[0]).wait()


def on_device(queries, keys, values, lengths, output_projection_weight):
    tokens = queries.shape[0]
    cores, halves = lax.axis_size("grp"), lax.axis_size("kv")
    lanes = cores * halves
    pairs = lax.axis_size("srv") // lanes
    assert cores == 2 and pairs == 2 and halves > 1 and lanes > EARLY
    groups, head = keys.shape[1], keys.shape[2]
    inner = groups * queries.shape[2]
    weight = output_projection_weight.reshape(inner, -1)
    columns = weight.shape[1]
    heads = inner // (groups * head)
    kvh = max(1, groups // pairs)
    hp = inner // head // pairs
    hpp = 2
    cw = max(256, columns // 2)
    own_chunks = columns // cw
    chunks = own_chunks * pairs
    items = lanes * pairs * chunks
    pieces = hp // hpp * pairs
    part = tokens // lanes
    back = REACH // pairs
    width = kvh * head
    dma = pltpu.SemaphoreType.DMA
    bf16, f32 = jnp.bfloat16, jnp.float32
    hbm = pl.BlockSpec(memory_space=pltpu.HBM)
    return pl.pallas_call(
        functools.partial(layer, (head, heads, kvh, hp, hpp, halves, lanes, pairs, cw)),
        out_shape=jax.ShapeDtypeStruct((tokens, pairs * columns), bf16),
        in_specs=[hbm] * 5,
        out_specs=pl.BlockSpec(memory_space=pl.ANY),
        scratch_shapes=[
            pltpu.SMEM(lengths.shape, lengths.dtype),
            pltpu.VMEM(queries.shape, bf16),
            pltpu.VMEM(keys.shape, bf16),
            pltpu.VMEM(values.shape, bf16),
            pltpu.VMEM((tokens, inner), bf16),
            pltpu.VMEM((2, tokens, groups * head), bf16),
            pltpu.VMEM((2, (back + 1) * pairs, tokens, width), bf16),
            pltpu.VMEM((pairs, tokens, hp * head), bf16),
            pltpu.VMEM((pairs, tokens, (REACH + 1) * tokens), f32),
            pltpu.VMEM((lanes, pairs, tokens, hp * head), bf16),
            pltpu.VMEM((chunks, hp * head, cw), bf16),
            pltpu.VMEM((items, tokens // cores, cw), f32),
            pltpu.VMEM((items, tokens // cores, cw), bf16),
            pltpu.VMEM((items, tokens // cores, cw), bf16),
            pltpu.VMEM((items, tokens // cores, cw), bf16),
            pltpu.VMEM((items, halves - 1, part, cw), bf16),
            pltpu.VMEM((lanes * chunks, part, cw), bf16),
            pltpu.VMEM((lanes * chunks, part, cw), bf16),
            pltpu.VMEM(((lanes - EARLY) * chunks, tokens // cores, cw), bf16),
            pltpu.VMEM((lanes * chunks, part, cw), bf16),
            dma((kvh,)), dma((kvh,)), dma((back, pairs, kvh)), dma((back, pairs, kvh)),
            dma((2 * back + 1, kvh)), dma((2 * back + 1, kvh)), dma((kvh,)), dma((kvh,)),
            dma((own_chunks,)), dma((own_chunks,)), dma((own_chunks,)),
            dma((2, lanes - 1)), dma((2, lanes - 1, pieces)),
            dma((1,)), dma((RING,)), dma((1,)), dma((2 * RING,)),
            dma((2,)), dma((lanes * chunks,)), dma((1,)), dma((1,)),
            dma((4,)),
        ],
        compiler_params=pltpu.CompilerParams(
            collective_id=0, has_side_effects=True, vmem_limit_bytes=52 * 1024 * 1024
        ),
    )(*[pltpu.with_memory_space_constraint(x, pltpu.HBM) for x in (lengths, queries, keys, values, weight)])


def solution(mesh):
    placed = (
        P("srv", "kv", "grp"),
        P("srv", "kv", None),
        P("srv", "kv", None),
        P(),
        P("kv", "grp", "srv"),
    )
    return jax.shard_map(
        on_device, mesh=mesh, in_specs=placed, out_specs=P("srv", ("grp", "kv")), check_vma=False
    )
```

```python
import functools
import math

import jax
import jax.numpy as jnp
from jax import lax
from jax.experimental import pallas as pl
from jax.experimental.pallas import tpu as pltpu
from jax.sharding import PartitionSpec as P

REACH = 4
EARLY = 3
FAR = -1e30
LAG = 5
RING = 8
MESH = pl.DeviceIdType.MESH


def layer(plan, lengths_in, q_hbm, k_hbm, v_hbm, w_ref, out_ref,
          lengths, q_in, k_in, v_in, q_ref, kv_ref, kvw, qbuf, bias, abuf, wbuf, acc,
          send1, recv1, send2, recv2, send3, recv3, far3, send4,
          ky_s, ky_r, kz_s, kz_r, sw_s, sw_r, q_s, q_r, own_w, w_s, w_r, a_s, a_r,
          s1, r1, s2, r2, s3, r3, s4, r4, in_s):
    head, heads, kvh, hp, hpp, halves, lanes, pairs, cw = plan
    tokens = q_ref.shape[0]
    inner = hp * head
    width = kvh * head
    split_kv = kv_ref.shape[2] > width
    own_chunks = w_ref.shape[1] // cw
    chunks = own_chunks * pairs
    items = lanes * pairs * chunks
    soon = own_chunks // 2
    segments = [(0, 2, 0, own_chunks), (0, 2, own_chunks, soon), (2, 1, 0, own_chunks + soon),
                (0, EARLY, own_chunks + soon, own_chunks - soon),
                (EARLY, lanes - EARLY, 0, chunks)]
    starts = [0]
    for _, planes, _, some in segments:
        starts.append(starts[-1] + planes * pairs * some)
    places = {}
    for (k0, planes, c0, some), n0 in zip(segments[:-1], starts):
        for r in range(planes * pairs * some):
            places[k0 + r // (pairs * some), r // some % pairs, c0 + r % some] = n0 + r
    swapped = (lanes - EARLY) * pairs * chunks
    ordered = list(range(chunks))
    partner = [(c + own_chunks) % chunks for c in ordered]
    last = [[(k, c) for k in range(EARLY) for c in range(chunks) if (c % own_chunks < soon) == kind]
            for kind in (True, False)]
    settle = [
        max([max(places[k, 1, c], places[k, 0, (c + own_chunks) % chunks]) + LAG + 1 - m
             for m, (k, c) in enumerate(some)] + [starts[3] + 2])
        for some in last
    ]
    settle.append(settle[1] + swapped)
    settle[1] = max(settle[1], settle[0] + len(last[0]))
    settle[2] = max(settle[2], settle[0] + len(last[0]))
    back = REACH // pairs
    pieces = hp // hpp * pairs
    piece = hpp * head
    per_kv = hp // kvh
    per_run = per_kv // hpp
    each = -(-pieces // 4)
    wait_for = own_chunks * pairs - 2 if own_chunks > 1 else 1
    part = tokens // lanes
    a, g, s = lax.axis_index("grp"), lax.axis_index("kv"), lax.axis_index("srv")
    u, v = s // pairs, s % pairs
    q = a * halves + g
    ov = 1 - v

    core = (1 - a, g, s)
    beside = (a, g, u * pairs + ov)
    ahead = (a, g, s + pairs)
    behind = (a, g, s - pairs)
    right, left = u + 1 < lanes, u > 0
    at_home = q == u

    def other_half(k):
        return (a, (g + k) % halves, s)

    def owner(p):
        return (u // halves, u % halves, p * pairs + v)

    def giver(p):
        return (p // halves, p % halves, q * pairs + v)

    arriving = [
        pltpu.make_async_copy(src, dst, in_s.at[i])
        for i, (src, dst) in enumerate(
            ((k_hbm, k_in), (v_hbm, v_in), (q_hbm, q_in), (lengths_in, lengths)))
    ]
    for copy in arriving:
        copy.start()

    barrier = pltpu.get_barrier_semaphore()

    def greet(device):
        pl.semaphore_signal(barrier, inc=1, device_id=device, device_id_type=MESH)

    greet(core)
    greet(beside)
    for k in range(1, halves):
        greet(other_half(k))
    pl.when(right)(lambda: greet(ahead))
    pl.when(left)(lambda: greet(behind))
    for p in range(lanes):
        pl.when(jnp.logical_not(at_home & (q == p)))(lambda p=p: greet(giver(p)))
    peers = jnp.int32(1 + halves + lanes)
    peers = peers + jnp.where(right, 1, 0) + jnp.where(left, 1, 0) - jnp.where(at_home, 1, 0)

    def remote(src, dst, send, recv, device):
        return pltpu.make_async_remote_copy(
            src_ref=src, dst_ref=dst, send_sem=send, recv_sem=recv,
            device_id=device, device_id_type=MESH,
        )

    def lane_at(i, size):
        return pl.ds(pl.multiple_of(i, head), size)

    def kv_from(half, j):
        offset = half * width + j * head if split_kv else j * head
        return kv_ref.at[a, :, lane_at(offset, head)]

    def kv_at(m, back_by, w, j):
        return kvw.at[m, (back - back_by) * pairs + w, :, pl.ds(j * head, head)]

    def whose(w):
        return v if w == 0 else ov

    def kv_beside(j):
        return remote(kv_from(ov, j), kv_at(a, 0, v, j), ky_s.at[j], ky_r.at[j], beside)

    def kv_came(j):
        return remote(kv_from(ov, j), kv_at(a, 0, ov, j), ky_s.at[j], ky_r.at[j], beside)

    def kv_up(d, w, j):
        src = kv_from(v, j) if d == 1 and w == 0 else kv_at(a, d - 1, whose(w), j)
        return remote(src, kv_at(a, d, whose(w), j), kz_s.at[d - 1, w, j], kz_r.at[d - 1, w, j],
                      ahead)

    def swap(d, w, j, m):
        i = 0 if d == 0 else 2 * d - 1 + w
        ref = kv_at(m, d, whose(w), j)
        return remote(ref, ref, sw_s.at[i, j], sw_r.at[i, j], core)

    def query(j):
        size = per_kv * head
        return remote(q_ref.at[:, lane_at(ov * inner + j * size, size)],
                      qbuf.at[0, :, pl.ds(j * size, size)], q_s.at[j], q_r.at[j], beside)

    def weight(c):
        return remote(w_ref.at[pl.ds(ov * inner, inner), pl.ds(c * cw, cw)],
                      wbuf.at[own_chunks + c], w_s.at[c], w_r.at[c], beside)

    def own_weight(c):
        return pltpu.make_async_copy(
            w_ref.at[pl.ds(v * inner, inner), pl.ds(c * cw, cw)], wbuf.at[c], own_w.at[c])

    for c in range(own_chunks):
        own_weight(c).start()

    arriving[0].wait()
    arriving[1].wait()
    for j in range(k_in.shape[1]):
        kv_ref[0, :, j * head:(j + 1) * head] = k_in[:, j]
        kv_ref[1, :, j * head:(j + 1) * head] = v_in[:, j]

    pl.semaphore_wait(barrier, peers)

    for j in range(kvh):
        kv_beside(j).start()
        pl.when(right)(lambda j=j: kv_up(1, 0, j).start())
    span = q_in.shape[2]
    arriving[2].wait()
    for j in range(q_in.shape[1]):
        q_ref[:, j * span:(j + 1) * span] = q_in[:, j]
    for j in range(kvh):
        query(j).start()
    for c in range(own_chunks):
        weight(c).start()

    for m in range(2):
        offset = v * width if split_kv else 0
        kvw[m, back * pairs + v] = kv_ref[m, :, lane_at(offset, width)]
    qbuf[1] = q_ref[:, lane_at(v * inner, inner)]
    for d in range(1, back + 1):
        @pl.when(u < d)
        def _():
            for m in range(2):
                for w in range(pairs):
                    kvw[m, (back - d) * pairs + w] = jnp.zeros((tokens, width), kvw.dtype)

    arriving[3].wait()
    row = lax.broadcasted_iota(jnp.int32, (tokens, 1), 0)
    lane = lax.broadcasted_iota(jnp.int32, (tokens, tokens), 1)
    for h in range(pairs):
        shard = u * pairs + (ov if h == 0 else v)
        query_pos = shard * tokens + row
        first = jnp.zeros((tokens, 1), jnp.int32)
        start = jnp.int32(0)
        for i in range(lengths.shape[0]):
            first = jnp.where(query_pos >= start, start, first)
            start = start + lengths[i]
        for d in range(REACH + 1):
            key_pos = (shard - REACH + d) * tokens + lane
            allowed = (key_pos >= first) & (key_pos <= query_pos)
            bias[h, :, d * tokens:(d + 1) * tokens] = jnp.where(allowed, 0.0, FAR)

    def kv_hop(d, j):
        @pl.when(u >= d)
        def _():
            for w in range(pairs):
                kv_up(d, w, j).wait_recv()
                if d < back:
                    pl.when(right)(lambda w=w: kv_up(d + 1, w, j).start())
                swap(d, w, j, a).start()

    def kv_phase(j):
        kv_came(j).wait_recv()
        pl.when(right)(lambda: kv_up(1, 1, j).start())
        swap(0, 1, j, a).start()
        for d in range(1, back):
            kv_hop(d, j)

    def kv_ready(j):
        swap(0, 1, j, 1 - a).wait_recv()
        for d in range(1, back + 1):
            @pl.when(u >= d)
            def _():
                for w in range(pairs):
                    swap(d, w, j, 1 - a).wait_recv()

    def run(b):
        return b // kvh, b % kvh

    def bit(p, i):
        h, j = run(i // per_run)
        r = j * per_run + i % per_run
        return abuf.at[p, jnp.where(h == 0, ov, v), :, lane_at(r * piece, piece)]

    def relay(way, d, i):
        p = u - (d - 1) if way == 0 else u + (d - 1)
        return remote(bit(p, i), bit(p, i), a_s.at[way, d - 1], a_r.at[way, d - 1, i],
                      ahead if way == 0 else behind)

    def relayed(way, d, i):
        p = u - d if way == 0 else u + d
        return remote(bit(p, i), bit(p, i), a_s.at[way, d - 1], a_r.at[way, d - 1, i],
                      behind if way == 0 else ahead)

    def holds(way, d):
        return u >= d if way == 0 else u + d < lanes

    def may_send(way):
        return right if way == 0 else left

    def forward(d, i):
        for way in range(2):
            @pl.when(holds(way, d - 1) & may_send(way))
            def _():
                relayed(way, d - 1, i).wait_recv()
                relay(way, d, i).start()

    factor = math.log2(math.e) / math.sqrt(head)
    for j in range(min(2, kvh)):
        kv_phase(j)
    kv_hop(back, 0)
    kv_ready(0)

    def per_unit(i):
        h, kj = run(i // per_kv)
        hh = kj * per_kv + i % per_kv
        vv = jnp.where(h == 0, ov, v)
        for j in range(kvh):
            if j > 0:
                if j > 1:
                    pl.when(i == (j - 1) * per_kv)(lambda: kv_phase(j))
                pl.when(i == j * per_kv - 1)(lambda: kv_hop(back, j))
                pl.when(i == j * per_kv)(lambda: kv_ready(j))
            pl.when(i == j * per_kv)(lambda: query(j).wait_recv())
        mine = lane_at(hh * head, head)
        at = lane_at(kj * head, head)
        window = kvw[0, pl.ds(vv, REACH + 1), :, at].reshape((REACH + 1) * tokens, head)
        scores = lax.dot_general(
            qbuf[h, :, mine], window, (((1,), (1,)), ((), ())),
            preferred_element_type=jnp.float32,
        ) + bias[h]
        peak = jnp.max(scores, axis=1, keepdims=True)
        weights = jnp.exp2((scores - peak) * factor)
        total = jnp.sum(weights, axis=1, keepdims=True)
        numer = jnp.dot(
            weights.astype(jnp.bfloat16),
            kvw[1, pl.ds(vv, REACH + 1), :, at].reshape((REACH + 1) * tokens, head),
            preferred_element_type=jnp.float32,
        )
        abuf[u, vv, :, mine] = (numer / total).astype(abuf.dtype)

        @pl.when(i % hpp == hpp - 1)
        def _():
            n = i // hpp
            for way in range(2):
                pl.when(may_send(way))(lambda: relay(way, 1, n).start())

    units = hp * pairs
    ahead_by = units - own_chunks - 1

    def plane(k):
        low = jnp.minimum(u, lanes - 1 - u)
        zigzag = jnp.where(k % 2 == 1, u - (k + 1) // 2, u + k // 2)
        line = jnp.where(u < lanes - 1 - u, k, lanes - 1 - k)
        return jnp.where(k <= 2 * low, zigzag, line)

    inside = left & right

    def pick(i, values):
        found = jnp.int32(values[0])
        for at, value in enumerate(values[1:], 1):
            found = jnp.where(i == at, value, found)
        return found

    def decode(n):
        k, h, c = jnp.int32(0), jnp.int32(0), jnp.int32(0)
        fresh = jnp.bool_(False)
        kept_in = n < items
        m = jnp.where(n < starts[3] + swapped, n + starts[4] - starts[3], n - swapped)
        n = jnp.where(inside & (n >= starts[3]) & (n < items), m, n)
        for (k0, planes, c0, some), n0 in zip(segments, starts):
            if planes * some == 0:
                continue
            r = n - n0
            here = r >= 0
            half, order = r // some % pairs, c0 + r % some
            if k0 == EARLY:
                order = jnp.where(half == 0, pick(r % some, ordered), pick(r % some, partner))
            k = jnp.where(here, k0 + r // (pairs * some), k)
            h = jnp.where(here, half, h)
            c = jnp.where(here, order, c)
            fresh = jnp.where(here, (r % some == 0) & (c0 == 0), fresh)
        return k, h, c, fresh & (k > 0) & kept_in

    def column(c):
        return jnp.where(c < own_chunks, v * own_chunks + c, ov * own_chunks + c - own_chunks)

    def to_core(n):
        return remote(send1.at[n], recv1.at[n], s1.at[0], r1.at[n % RING], core)

    def to_half(n, k):
        rows = pl.ds((g + k) % halves * part, part)
        return remote(send2.at[n, rows], recv2.at[n, k - 1], s2.at[0], r2.at[n % (2 * RING)], other_half(k))

    def all_halves(n):
        return remote(recv2.at[n], recv2.at[n], s2.at[0], r2.at[n % (2 * RING)], other_half(1))

    def to_beside(k, c):
        i = k * chunks + c
        return remote(send3.at[i], recv3.at[i], s3.at[0], r3.at[i], beside)

    def result(giver_index, c):
        return out_ref.at[pl.ds(giver_index * part, part), lane_at(c * cw, cw)]

    def to_owner(k, c):
        return remote(send4.at[k * chunks + c], result(q, c), s4.at[0], r4.at[0], owner(plane(k)))

    def to_self(c):
        return pltpu.make_async_copy(send4.at[c], result(q, c), r4.at[0])

    def stage1(n):
        k, h, c, _ = decode(n)
        product = jnp.dot(abuf[plane(k), jnp.where(h == 0, ov, v)], wbuf[c],
                          preferred_element_type=jnp.float32)
        low, high = product[:tokens // 2], product[tokens // 2:]
        acc[n] = jnp.where(a == 0, low, high)
        send1[n] = jnp.where(a == 0, high, low).astype(send1.dtype)
        to_core(n).start()

    def far_beside(k, c, n):
        return remote(send2.at[n], far3.at[(k - EARLY) * chunks + c], s3.at[1],
                      r3.at[k * chunks + c], beside)

    def to_halves(n, total):
        acc[n] = total
        send2[n] = total.astype(send2.dtype)
        for k in range(1, halves):
            to_half(n, k).start()

    def direct(k, c):
        return k >= EARLY

    def stage2(n):
        k, h, c, _ = decode(n)
        col = column(c)
        to_core(n).wait_recv()
        total = acc[n] + recv1[n].astype(jnp.float32)
        y_first = direct(k, c)
        pl.when(jnp.logical_not(y_first))(lambda: to_halves(n, total))

        @pl.when(y_first & (h == 0))
        def _():
            send2[n] = total.astype(send2.dtype)
            far_beside(k, col, n).start()

        @pl.when(y_first & (h != 0))
        def _():
            far_beside(k, col, n).wait_recv()
            to_halves(n, total + far3[(k - EARLY) * chunks + col].astype(jnp.float32))

    kept = pl.ds(g * part, part)

    def deliver(k, col, total):
        send4[k * chunks + col] = total.astype(send4.dtype)
        pl.when(at_home & (k == 0))(lambda: to_self(col).start())
        pl.when(jnp.logical_not(at_home & (k == 0)))(lambda: to_owner(k, col).start())

    def stage3(n):
        k, h, c, _ = decode(n)
        col = column(c)

        y_first = direct(k, c)

        @pl.when(jnp.logical_not(y_first) | (h != 0))
        def _():
            all_halves(n).wait_recv()
            total = acc[n, kept]
            for i in range(halves - 1):
                total = total + recv2[n, i].astype(jnp.float32)

            @pl.when(h == 0)
            def _():
                send3[k * chunks + col] = total.astype(send3.dtype)
                to_beside(k, col).start()

            @pl.when((h != 0) & (k < EARLY))
            def _():
                acc[n, kept] = total

            pl.when((h != 0) & y_first)(lambda: deliver(k, col, total))

            @pl.when((h != 0) & (k >= EARLY) & jnp.logical_not(y_first))
            def _():
                to_beside(k, col).wait_recv()
                deliver(k, col, total + recv3[k * chunks + col].astype(jnp.float32))

    def stage4(n, k, c):
        col = column(c)
        to_beside(k, col).wait_recv()
        deliver(k, col, acc[n, kept] + recv3[k * chunks + col].astype(jnp.float32))

    def arrived(k, h):
        p = plane(k)
        up = p < u
        d = jnp.where(up, u - p, p - u)
        way = jnp.where(up, 0, 1)

        @pl.when(jnp.logical_not(jnp.where(up, right, left)))
        def _():
            def one(r, carry):
                i = h * kvh * per_run + r
                remote(bit(p, i), bit(p, i), a_s.at[way, d - 1], a_r.at[way, d - 1, i],
                       core).wait_recv()
                return carry

            lax.fori_loop(0, kvh * per_run, one, 0)

    def per_item(n):
        k, h, c, fresh = decode(n)

        f = (n - wait_for) * each

        @pl.when((f >= 0) & (f < pieces))
        def _():
            for i in range(each):
                pl.when(f + i < pieces)(lambda i=i: forward(2, f + i))

        if lanes > 3:
            for i in range(pieces):
                at = starts[1] + (starts[3] - starts[1] + 1) * i // pieces
                pl.when(n == at)(lambda i=i: forward(3, i))
        if lanes > 4:
            @pl.when(n == starts[3])
            def _():
                for d in range(4, lanes):
                    def one(i, carry):
                        forward(d, i)
                        return carry

                    lax.fori_loop(0, pieces, one, 0)

        for i in range(own_chunks):
            used = starts[1] + i if i < soon else starts[3]
            pl.when(n == used)(lambda i=i: weight(i).wait_recv())
        done = decode(n - 1)[3]
        pl.when(fresh & jnp.logical_not(done) & (n >= 2))(lambda: stage2(n - 2))

        @pl.when(fresh)
        def _():
            stage2(n - 1)
            arrived(k, h)

        pl.when(n < items)(lambda: stage1(n))
        pending = jnp.logical_not(fresh | done) & (n >= 2 + own_chunks) & (n < items + 2)
        pl.when(pending)(lambda: stage2(n - 2))
        pl.when((n >= LAG) & (n < items + LAG))(lambda: stage3(n - LAG))
        later = jnp.where(inside, swapped, 0)
        index, mk, mc = jnp.int32(-1), jnp.int32(0), jnp.int32(0)
        begins = settle[0], jnp.where(inside, settle[2], settle[1])
        for some, first, shift in zip(last, begins, (0, later)):
            for m, (k1, c1) in enumerate(some):
                here = n == first + m
                held = places[k1, 1, c1]
                index = jnp.where(here, held + (shift if held >= starts[3] else 0), index)
                mk, mc = jnp.where(here, k1, mk), jnp.where(here, c1, mc)
        pl.when(index >= 0)(lambda: stage4(index, mk, mc))

    def step(i, carry):
        pl.when(i < units)(lambda: per_unit(i))
        for c in range(own_chunks):
            @pl.when(i == hp + 2 * c)
            def _():
                own_weight(c).wait()
                stage1(c)

            pl.when(i == hp + 2 * c + 1)(lambda: stage2(c))
        pl.when(i >= units - 1)(lambda: per_item(i - ahead_by))
        return carry

    lax.fori_loop(0, ahead_by + max(items + LAG, settle[2] + len(last[1])), step, 0)

    far = (lanes - EARLY) * chunks

    def sent(ref, sem):
        remote(ref, ref, sem, sem, core).wait_send()

    for j in range(kvh):
        kv_beside(j).wait_send()
        query(j).wait_send()
        swap(0, 1, j, a).wait_send()
        for d in range(1, back + 1):
            for w in range(pairs):
                pl.when((u >= d - 1) & right)(lambda d=d, w=w, j=j: kv_up(d, w, j).wait_send())
                pl.when(u >= d)(lambda d=d, w=w, j=j: swap(d, w, j, a).wait_send())
    for c in range(own_chunks):
        weight(c).wait_send()
    for d in range(1, lanes):
        for way in range(2):
            p = u - (d - 1) if way == 0 else u + (d - 1)
            pl.when(holds(way, d - 1) & may_send(way))(
                lambda p=p, way=way, d=d: sent(abuf.at[p], a_s.at[way, d - 1]))

    sent(send1, s1.at[0])
    sent(recv2.at[pl.ds(0, items - far)], s2.at[0])
    sent(send3.at[pl.ds(0, lanes * chunks - far)], s3.at[0])
    sent(far3.at[pl.ds(0, far)], s3.at[1])
    pl.when(at_home)(lambda: sent(send4.at[pl.ds(chunks, (lanes - 1) * chunks)], s4.at[0]))
    pl.when(jnp.logical_not(at_home))(lambda: sent(send4, s4.at[0]))
    pltpu.make_async_copy(out_ref, out_ref, r4.at[0]).wait()


def on_device(queries, keys, values, lengths, output_projection_weight):
    tokens = queries.shape[0]
    cores, halves = lax.axis_size("grp"), lax.axis_size("kv")
    lanes = cores * halves
    pairs = lax.axis_size("srv") // lanes
    assert cores == 2 and pairs == 2 and halves > 1 and lanes > EARLY
    groups, head = keys.shape[1], keys.shape[2]
    inner = groups * queries.shape[2]
    weight = output_projection_weight.reshape(inner, -1)
    columns = weight.shape[1]
    heads = inner // (groups * head)
    kvh = max(1, groups // pairs)
    hp = inner // head // pairs
    hpp = 2
    cw = max(256, columns // 2)
    own_chunks = columns // cw
    chunks = own_chunks * pairs
    items = lanes * pairs * chunks
    pieces = hp // hpp * pairs
    part = tokens // lanes
    back = REACH // pairs
    width = kvh * head
    dma = pltpu.SemaphoreType.DMA
    bf16, f32 = jnp.bfloat16, jnp.float32
    hbm = pl.BlockSpec(memory_space=pltpu.HBM)
    return pl.pallas_call(
        functools.partial(layer, (head, heads, kvh, hp, hpp, halves, lanes, pairs, cw)),
        out_shape=jax.ShapeDtypeStruct((tokens, pairs * columns), bf16),
        in_specs=[hbm] * 5,
        out_specs=pl.BlockSpec(memory_space=pl.ANY),
        scratch_shapes=[
            pltpu.SMEM(lengths.shape, lengths.dtype),
            pltpu.VMEM(queries.shape, bf16),
            pltpu.VMEM(keys.shape, bf16),
            pltpu.VMEM(values.shape, bf16),
            pltpu.VMEM((tokens, inner), bf16),
            pltpu.VMEM((2, tokens, groups * head), bf16),
            pltpu.VMEM((2, (back + 1) * pairs, tokens, width), bf16),
            pltpu.VMEM((pairs, tokens, hp * head), bf16),
            pltpu.VMEM((pairs, tokens, (REACH + 1) * tokens), f32),
            pltpu.VMEM((lanes, pairs, tokens, hp * head), bf16),
            pltpu.VMEM((chunks, hp * head, cw), bf16),
            pltpu.VMEM((items, tokens // cores, cw), f32),
            pltpu.VMEM((items, tokens // cores, cw), bf16),
            pltpu.VMEM((items, tokens // cores, cw), bf16),
            pltpu.VMEM((items, tokens // cores, cw), bf16),
            pltpu.VMEM((items, halves - 1, part, cw), bf16),
            pltpu.VMEM((lanes * chunks, part, cw), bf16),
            pltpu.VMEM((lanes * chunks, part, cw), bf16),
            pltpu.VMEM(((lanes - EARLY) * chunks, tokens // cores, cw), bf16),
            pltpu.VMEM((lanes * chunks, part, cw), bf16),
            dma((kvh,)), dma((kvh,)), dma((back, pairs, kvh)), dma((back, pairs, kvh)),
            dma((2 * back + 1, kvh)), dma((2 * back + 1, kvh)), dma((kvh,)), dma((kvh,)),
            dma((own_chunks,)), dma((own_chunks,)), dma((own_chunks,)),
            dma((2, lanes - 1)), dma((2, lanes - 1, pieces)),
            dma((1,)), dma((RING,)), dma((1,)), dma((2 * RING,)),
            dma((2,)), dma((lanes * chunks,)), dma((1,)), dma((1,)),
            dma((4,)),
        ],
        compiler_params=pltpu.CompilerParams(
            collective_id=0, has_side_effects=True, vmem_limit_bytes=52 * 1024 * 1024
        ),
    )(*[pltpu.with_memory_space_constraint(x, pltpu.HBM) for x in (lengths, queries, keys, values, weight)])


def solution(mesh):
    placed = (
        P("srv", "kv", "grp"),
        P("srv", "kv", None),
        P("srv", "kv", None),
        P(),
        P("kv", "grp", "srv"),
    )
    return jax.shard_map(
        on_device, mesh=mesh, in_specs=placed, out_specs=P("srv", ("grp", "kv")), check_vma=False
    )
```

```python
import functools
import math

import jax
import jax.numpy as jnp
from jax import lax
from jax.experimental import pallas as pl
from jax.experimental.pallas import tpu as pltpu
from jax.sharding import PartitionSpec as P

REACH = 4
EARLY = 3
FAR = -1e30
LAG = 5
RING = 8
MESH = pl.DeviceIdType.MESH


def layer(plan, lengths_in, q_hbm, k_hbm, v_hbm, w_ref, out_ref,
          lengths, q_in, k_in, v_in, q_ref, kv_ref, kvw, qbuf, bias, abuf, wbuf, acc,
          send1, recv1, send2, recv2, send3, recv3, far3, send4,
          ky_s, ky_r, kz_s, kz_r, sw_s, sw_r, q_s, q_r, own_w, w_s, w_r, a_s, a_r,
          s1, r1, s2, r2, s3, r3, s4, r4, in_s):
    head, heads, kvh, hp, hpp, halves, lanes, pairs, cw = plan
    tokens = q_ref.shape[0]
    inner = hp * head
    width = kvh * head
    split_kv = kv_ref.shape[2] > width
    own_chunks = w_ref.shape[1] // cw
    chunks = own_chunks * pairs
    items = lanes * pairs * chunks
    soon = own_chunks // 2
    segments = [(0, 2, 0, own_chunks), (0, 2, own_chunks, soon), (2, 1, 0, own_chunks + soon),
                (0, EARLY, own_chunks + soon, own_chunks - soon),
                (EARLY, lanes - EARLY, 0, chunks)]
    starts = [0]
    for _, planes, _, some in segments:
        starts.append(starts[-1] + planes * pairs * some)
    places = {}
    for (k0, planes, c0, some), n0 in zip(segments[:-1], starts):
        for r in range(planes * pairs * some):
            places[k0 + r // (pairs * some), r // some % pairs, c0 + r % some] = n0 + r
    swapped = (lanes - EARLY) * pairs * chunks
    ordered = list(range(chunks))
    partner = [(c + own_chunks) % chunks for c in ordered]
    last = [[(k, c) for k in range(EARLY) for c in range(chunks) if (c % own_chunks < soon) == kind]
            for kind in (True, False)]
    settle = [
        max([max(places[k, 1, c], places[k, 0, (c + own_chunks) % chunks]) + LAG + 1 - m
             for m, (k, c) in enumerate(some)] + [starts[3] + 2])
        for some in last
    ]
    settle.append(settle[1] + swapped)
    settle[1] = max(settle[1], settle[0] + len(last[0]))
    settle[2] = max(settle[2], settle[0] + len(last[0]))
    back = REACH // pairs
    pieces = hp // hpp * pairs
    piece = hpp * head
    per_kv = hp // kvh
    per_run = per_kv // hpp
    each = -(-pieces // 4)
    wait_for = own_chunks * pairs - 2 if own_chunks > 1 else 1
    part = tokens // lanes
    a, g, s = lax.axis_index("grp"), lax.axis_index("kv"), lax.axis_index("srv")
    u, v = s // pairs, s % pairs
    q = a * halves + g
    ov = 1 - v

    core = (1 - a, g, s)
    beside = (a, g, u * pairs + ov)
    ahead = (a, g, s + pairs)
    behind = (a, g, s - pairs)
    right, left = u + 1 < lanes, u > 0
    at_home = q == u

    def other_half(k):
        return (a, (g + k) % halves, s)

    def owner(p):
        return (u // halves, u % halves, p * pairs + v)

    def giver(p):
        return (p // halves, p % halves, q * pairs + v)

    arriving = [
        pltpu.make_async_copy(src, dst, in_s.at[i])
        for i, (src, dst) in enumerate(
            ((k_hbm, k_in), (v_hbm, v_in), (q_hbm, q_in), (lengths_in, lengths)))
    ]
    for copy in arriving:
        copy.start()

    barrier = pltpu.get_barrier_semaphore()

    def greet(device):
        pl.semaphore_signal(barrier, inc=1, device_id=device, device_id_type=MESH)

    greet(core)
    greet(beside)
    for k in range(1, halves):
        greet(other_half(k))
    pl.when(right)(lambda: greet(ahead))
    pl.when(left)(lambda: greet(behind))
    for p in range(lanes):
        pl.when(jnp.logical_not(at_home & (q == p)))(lambda p=p: greet(giver(p)))
    peers = jnp.int32(1 + halves + lanes)
    peers = peers + jnp.where(right, 1, 0) + jnp.where(left, 1, 0) - jnp.where(at_home, 1, 0)

    def remote(src, dst, send, recv, device):
        return pltpu.make_async_remote_copy(
            src_ref=src, dst_ref=dst, send_sem=send, recv_sem=recv,
            device_id=device, device_id_type=MESH,
        )

    def lane_at(i, size):
        return pl.ds(pl.multiple_of(i, head), size)

    def kv_from(half, j):
        offset = half * width + j * head if split_kv else j * head
        return kv_ref.at[a, :, lane_at(offset, head)]

    def kv_at(m, back_by, w, j):
        return kvw.at[m, (back - back_by) * pairs + w, :, pl.ds(j * head, head)]

    def whose(w):
        return v if w == 0 else ov

    def kv_beside(j):
        return remote(kv_from(ov, j), kv_at(a, 0, v, j), ky_s.at[j], ky_r.at[j], beside)

    def kv_came(j):
        return remote(kv_from(ov, j), kv_at(a, 0, ov, j), ky_s.at[j], ky_r.at[j], beside)

    def kv_up(d, w, j):
        src = kv_from(v, j) if d == 1 and w == 0 else kv_at(a, d - 1, whose(w), j)
        return remote(src, kv_at(a, d, whose(w), j), kz_s.at[d - 1, w, j], kz_r.at[d - 1, w, j],
                      ahead)

    def swap(d, w, j, m):
        i = 0 if d == 0 else 2 * d - 1 + w
        ref = kv_at(m, d, whose(w), j)
        return remote(ref, ref, sw_s.at[i, j], sw_r.at[i, j], core)

    def query(j):
        size = per_kv * head
        return remote(q_ref.at[:, lane_at(ov * inner + j * size, size)],
                      qbuf.at[0, :, pl.ds(j * size, size)], q_s.at[0], q_r.at[j], beside)

    def weight(c):
        return remote(w_ref.at[pl.ds(ov * inner, inner), pl.ds(c * cw, cw)],
                      wbuf.at[own_chunks + c], w_s.at[0], w_r.at[c], beside)

    def own_weight(c):
        return pltpu.make_async_copy(
            w_ref.at[pl.ds(v * inner, inner), pl.ds(c * cw, cw)], wbuf.at[c], own_w.at[c])

    for c in range(own_chunks):
        own_weight(c).start()

    arriving[0].wait()
    arriving[1].wait()
    for j in range(k_in.shape[1]):
        kv_ref[0, :, j * head:(j + 1) * head] = k_in[:, j]
        kv_ref[1, :, j * head:(j + 1) * head] = v_in[:, j]

    pl.semaphore_wait(barrier, peers)

    for j in range(kvh):
        kv_beside(j).start()
        pl.when(right)(lambda j=j: kv_up(1, 0, j).start())
    span = q_in.shape[2]
    arriving[2].wait()
    for j in range(q_in.shape[1]):
        q_ref[:, j * span:(j + 1) * span] = q_in[:, j]
    for j in range(kvh):
        query(j).start()
    for c in range(own_chunks):
        weight(c).start()

    for m in range(2):
        offset = v * width if split_kv else 0
        kvw[m, back * pairs + v] = kv_ref[m, :, lane_at(offset, width)]
    qbuf[1] = q_ref[:, lane_at(v * inner, inner)]
    for d in range(1, back + 1):
        @pl.when(u < d)
        def _():
            for m in range(2):
                for w in range(pairs):
                    kvw[m, (back - d) * pairs + w] = jnp.zeros((tokens, width), kvw.dtype)

    arriving[3].wait()
    row = lax.broadcasted_iota(jnp.int32, (tokens, 1), 0)
    lane = lax.broadcasted_iota(jnp.int32, (tokens, tokens), 1)
    for h in range(pairs):
        shard = u * pairs + (ov if h == 0 else v)
        query_pos = shard * tokens + row
        first = jnp.zeros((tokens, 1), jnp.int32)
        start = jnp.int32(0)
        for i in range(lengths.shape[0]):
            first = jnp.where(query_pos >= start, start, first)
            start = start + lengths[i]
        for d in range(REACH + 1):
            key_pos = (shard - REACH + d) * tokens + lane
            allowed = (key_pos >= first) & (key_pos <= query_pos)
            bias[h, :, d * tokens:(d + 1) * tokens] = jnp.where(allowed, 0.0, FAR)

    def kv_hop(d, j):
        @pl.when(u >= d)
        def _():
            for w in range(pairs):
                kv_up(d, w, j).wait_recv()
                if d < back:
                    pl.when(right)(lambda w=w: kv_up(d + 1, w, j).start())
                swap(d, w, j, a).start()

    def kv_phase(j):
        kv_came(j).wait_recv()
        pl.when(right)(lambda: kv_up(1, 1, j).start())
        swap(0, 1, j, a).start()
        for d in range(1, back):
            kv_hop(d, j)

    def kv_ready(j):
        swap(0, 1, j, 1 - a).wait_recv()
        for d in range(1, back + 1):
            @pl.when(u >= d)
            def _():
                for w in range(pairs):
                    swap(d, w, j, 1 - a).wait_recv()

    def run(b):
        return b // kvh, b % kvh

    def bit(p, i):
        h, j = run(i // per_run)
        r = j * per_run + i % per_run
        return abuf.at[p, jnp.where(h == 0, ov, v), :, lane_at(r * piece, piece)]

    def relay(way, d, i):
        p = u - (d - 1) if way == 0 else u + (d - 1)
        return remote(bit(p, i), bit(p, i), a_s.at[way, d - 1], a_r.at[way, d - 1, i],
                      ahead if way == 0 else behind)

    def relayed(way, d, i):
        p = u - d if way == 0 else u + d
        return remote(bit(p, i), bit(p, i), a_s.at[way, d - 1], a_r.at[way, d - 1, i],
                      behind if way == 0 else ahead)

    def holds(way, d):
        return u >= d if way == 0 else u + d < lanes

    def may_send(way):
        return right if way == 0 else left

    def forward(d, i):
        for way in range(2):
            @pl.when(holds(way, d - 1) & may_send(way))
            def _():
                relayed(way, d - 1, i).wait_recv()
                relay(way, d, i).start()

    factor = math.log2(math.e) / math.sqrt(head)
    for j in range(min(2, kvh)):
        kv_phase(j)
    kv_hop(back, 0)
    kv_ready(0)

    def per_unit(i):
        h, kj = run(i // per_kv)
        hh = kj * per_kv + i % per_kv
        vv = jnp.where(h == 0, ov, v)
        for j in range(kvh):
            if j > 0:
                if j > 1:
                    pl.when(i == (j - 1) * per_kv)(lambda: kv_phase(j))
                pl.when(i == j * per_kv - 1)(lambda: kv_hop(back, j))
                pl.when(i == j * per_kv)(lambda: kv_ready(j))
            pl.when(i == j * per_kv)(lambda: query(j).wait_recv())
        mine = lane_at(hh * head, head)
        at = lane_at(kj * head, head)
        window = kvw[0, pl.ds(vv, REACH + 1), :, at].reshape((REACH + 1) * tokens, head)
        scores = lax.dot_general(
            qbuf[h, :, mine], window, (((1,), (1,)), ((), ())),
            preferred_element_type=jnp.float32,
        ) + bias[h]
        peak = jnp.max(scores, axis=1, keepdims=True)
        weights = jnp.exp2((scores - peak) * factor)
        total = jnp.sum(weights, axis=1, keepdims=True)
        numer = jnp.dot(
            weights.astype(jnp.bfloat16),
            kvw[1, pl.ds(vv, REACH + 1), :, at].reshape((REACH + 1) * tokens, head),
            preferred_element_type=jnp.float32,
        )
        abuf[u, vv, :, mine] = (numer / total).astype(abuf.dtype)

        @pl.when(i % hpp == hpp - 1)
        def _():
            n = i // hpp
            for way in range(2):
                pl.when(may_send(way))(lambda: relay(way, 1, n).start())

    units = hp * pairs
    ahead_by = units - own_chunks - 1

    def plane(k):
        low = jnp.minimum(u, lanes - 1 - u)
        zigzag = jnp.where(k % 2 == 1, u - (k + 1) // 2, u + k // 2)
        line = jnp.where(u < lanes - 1 - u, k, lanes - 1 - k)
        return jnp.where(k <= 2 * low, zigzag, line)

    inside = left & right

    def pick(i, values):
        found = jnp.int32(values[0])
        for at, value in enumerate(values[1:], 1):
            found = jnp.where(i == at, value, found)
        return found

    def decode(n):
        k, h, c = jnp.int32(0), jnp.int32(0), jnp.int32(0)
        fresh = jnp.bool_(False)
        kept_in = n < items
        m = jnp.where(n < starts[3] + swapped, n + starts[4] - starts[3], n - swapped)
        n = jnp.where(inside & (n >= starts[3]) & (n < items), m, n)
        for (k0, planes, c0, some), n0 in zip(segments, starts):
            if planes * some == 0:
                continue
            r = n - n0
            here = r >= 0
            half, order = r // some % pairs, c0 + r % some
            if k0 == EARLY:
                order = jnp.where(half == 0, pick(r % some, ordered), pick(r % some, partner))
            k = jnp.where(here, k0 + r // (pairs * some), k)
            h = jnp.where(here, half, h)
            c = jnp.where(here, order, c)
            fresh = jnp.where(here, (r % some == 0) & (c0 == 0), fresh)
        return k, h, c, fresh & (k > 0) & kept_in

    def column(c):
        return jnp.where(c < own_chunks, v * own_chunks + c, ov * own_chunks + c - own_chunks)

    def to_core(n):
        return remote(send1.at[n], recv1.at[n], s1.at[0], r1.at[n % RING], core)

    def to_half(n, k):
        rows = pl.ds((g + k) % halves * part, part)
        return remote(send2.at[n, rows], recv2.at[n, k - 1], s2.at[0], r2.at[n % (2 * RING)], other_half(k))

    def all_halves(n):
        return remote(recv2.at[n], recv2.at[n], s2.at[0], r2.at[n % (2 * RING)], other_half(1))

    def to_beside(k, c):
        i = k * chunks + c
        return remote(send3.at[i], recv3.at[i], s3.at[0], r3.at[i], beside)

    def result(giver_index, c):
        return out_ref.at[pl.ds(giver_index * part, part), lane_at(c * cw, cw)]

    def to_owner(k, c):
        return remote(send4.at[k * chunks + c], result(q, c), s4.at[0], r4.at[0], owner(plane(k)))

    def to_self(c):
        return pltpu.make_async_copy(send4.at[c], result(q, c), r4.at[0])

    def stage1(n):
        k, h, c, _ = decode(n)
        product = jnp.dot(abuf[plane(k), jnp.where(h == 0, ov, v)], wbuf[c],
                          preferred_element_type=jnp.float32)
        low, high = product[:tokens // 2], product[tokens // 2:]
        acc[n] = jnp.where(a == 0, low, high)
        send1[n] = jnp.where(a == 0, high, low).astype(send1.dtype)
        to_core(n).start()

    def far_beside(k, c, n):
        return remote(send2.at[n], far3.at[(k - EARLY) * chunks + c], s3.at[1],
                      r3.at[k * chunks + c], beside)

    def to_halves(n, total):
        acc[n] = total
        send2[n] = total.astype(send2.dtype)
        for k in range(1, halves):
            to_half(n, k).start()

    def direct(k, c):
        return k >= EARLY

    def stage2(n):
        k, h, c, _ = decode(n)
        col = column(c)
        to_core(n).wait_recv()
        total = acc[n] + recv1[n].astype(jnp.float32)
        y_first = direct(k, c)
        pl.when(jnp.logical_not(y_first))(lambda: to_halves(n, total))

        @pl.when(y_first & (h == 0))
        def _():
            send2[n] = total.astype(send2.dtype)
            far_beside(k, col, n).start()

        @pl.when(y_first & (h != 0))
        def _():
            far_beside(k, col, n).wait_recv()
            to_halves(n, total + far3[(k - EARLY) * chunks + col].astype(jnp.float32))

    kept = pl.ds(g * part, part)

    def deliver(k, col, total):
        send4[k * chunks + col] = total.astype(send4.dtype)
        pl.when(at_home & (k == 0))(lambda: to_self(col).start())
        pl.when(jnp.logical_not(at_home & (k == 0)))(lambda: to_owner(k, col).start())

    def stage3(n):
        k, h, c, _ = decode(n)
        col = column(c)

        y_first = direct(k, c)

        @pl.when(jnp.logical_not(y_first) | (h != 0))
        def _():
            all_halves(n).wait_recv()
            total = acc[n, kept]
            for i in range(halves - 1):
                total = total + recv2[n, i].astype(jnp.float32)

            @pl.when(h == 0)
            def _():
                send3[k * chunks + col] = total.astype(send3.dtype)
                to_beside(k, col).start()

            @pl.when((h != 0) & (k < EARLY))
            def _():
                acc[n, kept] = total

            pl.when((h != 0) & y_first)(lambda: deliver(k, col, total))

            @pl.when((h != 0) & (k >= EARLY) & jnp.logical_not(y_first))
            def _():
                to_beside(k, col).wait_recv()
                deliver(k, col, total + recv3[k * chunks + col].astype(jnp.float32))

    def stage4(n, k, c):
        col = column(c)
        to_beside(k, col).wait_recv()
        deliver(k, col, acc[n, kept] + recv3[k * chunks + col].astype(jnp.float32))

    def arrived(k, h):
        p = plane(k)
        up = p < u
        d = jnp.where(up, u - p, p - u)
        way = jnp.where(up, 0, 1)

        @pl.when(jnp.logical_not(jnp.where(up, right, left)))
        def _():
            def one(r, carry):
                i = h * kvh * per_run + r
                remote(bit(p, i), bit(p, i), a_s.at[way, d - 1], a_r.at[way, d - 1, i],
                       core).wait_recv()
                return carry

            lax.fori_loop(0, kvh * per_run, one, 0)

    def per_item(n):
        k, h, c, fresh = decode(n)

        f = (n - wait_for) * each

        @pl.when((f >= 0) & (f < pieces))
        def _():
            for i in range(each):
                pl.when(f + i < pieces)(lambda i=i: forward(2, f + i))

        if lanes > 3:
            for i in range(pieces):
                at = starts[1] + (starts[3] - starts[1] + 1) * i // pieces
                pl.when(n == at)(lambda i=i: forward(3, i))
        if lanes > 4:
            @pl.when(n == starts[3])
            def _():
                for d in range(4, lanes):
                    def one(i, carry):
                        forward(d, i)
                        return carry

                    lax.fori_loop(0, pieces, one, 0)

        for i in range(own_chunks):
            used = starts[1] + i if i < soon else starts[3]
            pl.when(n == used)(lambda i=i: weight(i).wait_recv())
        done = decode(n - 1)[3]
        pl.when(fresh & jnp.logical_not(done) & (n >= 2))(lambda: stage2(n - 2))

        @pl.when(fresh)
        def _():
            stage2(n - 1)
            arrived(k, h)

        pl.when(n < items)(lambda: stage1(n))
        pending = jnp.logical_not(fresh | done) & (n >= 2 + own_chunks) & (n < items + 2)
        pl.when(pending)(lambda: stage2(n - 2))
        pl.when((n >= LAG) & (n < items + LAG))(lambda: stage3(n - LAG))
        later = jnp.where(inside, swapped, 0)
        index, mk, mc = jnp.int32(-1), jnp.int32(0), jnp.int32(0)
        begins = settle[0], jnp.where(inside, settle[2], settle[1])
        for some, first, shift in zip(last, begins, (0, later)):
            for m, (k1, c1) in enumerate(some):
                here = n == first + m
                held = places[k1, 1, c1]
                index = jnp.where(here, held + (shift if held >= starts[3] else 0), index)
                mk, mc = jnp.where(here, k1, mk), jnp.where(here, c1, mc)
        pl.when(index >= 0)(lambda: stage4(index, mk, mc))

    def step(i, carry):
        pl.when(i < units)(lambda: per_unit(i))
        for c in range(own_chunks):
            @pl.when(i == hp + 2 * c)
            def _():
                own_weight(c).wait()
                stage1(c)

            pl.when(i == hp + 2 * c + 1)(lambda: stage2(c))
        pl.when(i >= units - 1)(lambda: per_item(i - ahead_by))
        return carry

    lax.fori_loop(0, ahead_by + max(items + LAG, settle[2] + len(last[1])), step, 0)

    far = (lanes - EARLY) * chunks

    def sent(ref, sem):
        remote(ref, ref, sem, sem, core).wait_send()

    for j in range(kvh):
        kv_beside(j).wait_send()
        swap(0, 1, j, a).wait_send()
        for d in range(1, back + 1):
            for w in range(pairs):
                pl.when((u >= d - 1) & right)(lambda d=d, w=w, j=j: kv_up(d, w, j).wait_send())
                pl.when(u >= d)(lambda d=d, w=w, j=j: swap(d, w, j, a).wait_send())
    sent(qbuf.at[0], q_s.at[0])
    sent(wbuf.at[pl.ds(0, own_chunks)], w_s.at[0])
    for d in range(1, lanes):
        for way in range(2):
            p = u - (d - 1) if way == 0 else u + (d - 1)
            pl.when(holds(way, d - 1) & may_send(way))(
                lambda p=p, way=way, d=d: sent(abuf.at[p], a_s.at[way, d - 1]))

    sent(send1, s1.at[0])
    sent(recv2.at[pl.ds(0, items - far)], s2.at[0])
    sent(send3.at[pl.ds(0, lanes * chunks - far)], s3.at[0])
    sent(far3.at[pl.ds(0, far)], s3.at[1])
    pl.when(at_home)(lambda: sent(send4.at[pl.ds(chunks, (lanes - 1) * chunks)], s4.at[0]))
    pl.when(jnp.logical_not(at_home))(lambda: sent(send4, s4.at[0]))
    pltpu.make_async_copy(out_ref, out_ref, r4.at[0]).wait()


def on_device(queries, keys, values, lengths, output_projection_weight):
    tokens = queries.shape[0]
    cores, halves = lax.axis_size("grp"), lax.axis_size("kv")
    lanes = cores * halves
    pairs = lax.axis_size("srv") // lanes
    assert cores == 2 and pairs == 2 and halves > 1 and lanes > EARLY
    groups, head = keys.shape[1], keys.shape[2]
    inner = groups * queries.shape[2]
    weight = output_projection_weight.reshape(inner, -1)
    columns = weight.shape[1]
    heads = inner // (groups * head)
    kvh = max(1, groups // pairs)
    hp = inner // head // pairs
    hpp = 2
    cw = max(256, columns // 2)
    own_chunks = columns // cw
    chunks = own_chunks * pairs
    items = lanes * pairs * chunks
    pieces = hp // hpp * pairs
    part = tokens // lanes
    back = REACH // pairs
    width = kvh * head
    dma = pltpu.SemaphoreType.DMA
    bf16, f32 = jnp.bfloat16, jnp.float32
    hbm = pl.BlockSpec(memory_space=pltpu.HBM)
    return pl.pallas_call(
        functools.partial(layer, (head, heads, kvh, hp, hpp, halves, lanes, pairs, cw)),
        out_shape=jax.ShapeDtypeStruct((tokens, pairs * columns), bf16),
        in_specs=[hbm] * 5,
        out_specs=pl.BlockSpec(memory_space=pl.ANY),
        scratch_shapes=[
            pltpu.SMEM(lengths.shape, lengths.dtype),
            pltpu.VMEM(queries.shape, bf16),
            pltpu.VMEM(keys.shape, bf16),
            pltpu.VMEM(values.shape, bf16),
            pltpu.VMEM((tokens, inner), bf16),
            pltpu.VMEM((2, tokens, groups * head), bf16),
            pltpu.VMEM((2, (back + 1) * pairs, tokens, width), bf16),
            pltpu.VMEM((pairs, tokens, hp * head), bf16),
            pltpu.VMEM((pairs, tokens, (REACH + 1) * tokens), f32),
            pltpu.VMEM((lanes, pairs, tokens, hp * head), bf16),
            pltpu.VMEM((chunks, hp * head, cw), bf16),
            pltpu.VMEM((items, tokens // cores, cw), f32),
            pltpu.VMEM((items, tokens // cores, cw), bf16),
            pltpu.VMEM((items, tokens // cores, cw), bf16),
            pltpu.VMEM((items, tokens // cores, cw), bf16),
            pltpu.VMEM((items, halves - 1, part, cw), bf16),
            pltpu.VMEM((lanes * chunks, part, cw), bf16),
            pltpu.VMEM((lanes * chunks, part, cw), bf16),
            pltpu.VMEM(((lanes - EARLY) * chunks, tokens // cores, cw), bf16),
            pltpu.VMEM((lanes * chunks, part, cw), bf16),
            dma((kvh,)), dma((kvh,)), dma((back, pairs, kvh)), dma((back, pairs, kvh)),
            dma((2 * back + 1, kvh)), dma((2 * back + 1, kvh)), dma((1,)), dma((kvh,)),
            dma((own_chunks,)), dma((1,)), dma((own_chunks,)),
            dma((2, lanes - 1)), dma((2, lanes - 1, pieces)),
            dma((1,)), dma((RING,)), dma((1,)), dma((2 * RING,)),
            dma((2,)), dma((lanes * chunks,)), dma((1,)), dma((1,)),
            dma((4,)),
        ],
        compiler_params=pltpu.CompilerParams(
            collective_id=0, has_side_effects=True, vmem_limit_bytes=52 * 1024 * 1024
        ),
    )(*[pltpu.with_memory_space_constraint(x, pltpu.HBM) for x in (lengths, queries, keys, values, weight)])


def solution(mesh):
    placed = (
        P("srv", "kv", "grp"),
        P("srv", "kv", None),
        P("srv", "kv", None),
        P(),
        P("kv", "grp", "srv"),
    )
    return jax.shard_map(
        on_device, mesh=mesh, in_specs=placed, out_specs=P("srv", ("grp", "kv")), check_vma=False
    )
```
